32 devices in a mesh: segment: 2 (over core), seq: 8 (over z, x), head: 2 (over y).
Axes of the slice: x: 2, y: 2, z: 4, core: 2. Of those that a mesh axis runs over, the one named last changes fastest.
Arguments:
- stream_in: bfloat16 [2, 2048, 3072], P('segment', 'seq'), may hold values from -6 to 6
- queries: bfloat16 [2, 2048, 1536], P('segment', 'seq', 'head'), may hold values from -8 to 8
- keys: bfloat16 [2, 2048, 1536], P('segment', 'seq', 'head'), may hold values from -8 to 8
- values: bfloat16 [2, 2048, 1536], P('segment', 'seq', 'head'), may hold values from -6 to 6
- out_weight: bfloat16 [2, 1536, 3072], P('segment', 'head'), may hold values from -0.15625 to 0.15625
- gate_scale: float32 [2, 3072], P('segment'), may hold values from 0.5 to 2
Outputs:
- stream_out: bfloat16 [2, 2048, 3072], P('segment', 'seq', 'head')
The draws below stay inside these ranges and needn't reach their ends.
All inputs are finite; a program needn't handle non-finite values.
Results may differ from the reference program's by a relative error of at most 0.0065.
Values may be sent and summed in bfloat16 or wider, within the bound.
No kernel may reach another device: no remote copies, remote signals or barrier semaphores. Data moves between devices by JAX's collectives and lax.ppermute only.
A program may use at most 64 MiB of HBM per device.

```python
import math
import jax
import jax.numpy as jnp
from jax import lax

D = 3072
HEADS = 12
HD = 128
TOK_DEV = 256
CYCLE = 8
VIDEOS = 1
SEQ = 2048
TOKENS = 2048
MICRO = 2


def shared_pair(key):
    base_key = jax.random.fold_in(key, 7)
    key_query, key_key = jax.random.split(base_key, 2)
    shape_all = (MICRO, TOKENS, HEADS * HD)
    query_draw = jnp.clip(jax.random.normal(key_query, shape_all, jnp.float32) * 1.6, -8.0, 8.0)
    key_draw = jnp.clip(jax.random.normal(key_key, shape_all, jnp.float32) * 1.6, -8.0, 8.0)
    return (query_draw, key_draw)


def draw_queries(key, part):
    return shared_pair(key)[0].astype(jnp.bfloat16)


def draw_keys(key, part):
    return shared_pair(key)[1].astype(jnp.bfloat16)


def steps_of(own_key, dims, shards, least, top_value):
    gain = 1.0
    for dim, blocks in shards:
        heights = jax.random.uniform(jax.random.fold_in(jax.random.fold_in(own_key, 6), dim), (blocks,), jnp.float32, least / len(shards), top_value / len(shards))
        gain = gain * jnp.repeat(jnp.exp(heights), dims[dim] // blocks).reshape((-1,) + (1,) * (len(dims) - 1 - dim))
    return gain


def scatter_about(key, extent, scale, most, cuts=(), held_as=jnp.bfloat16):
    result = jax.random.normal(key, extent, jnp.float32) * scale
    if len(cuts) > 0:
        result = steps_of(key, extent, cuts, -0.22, 0.18) * result
    return jnp.clip(result, min=-most, max=most).astype(held_as)


def setup_inputs(seed: int = 0) -> dict:
    key_of = jax.random.split(jax.random.key(seed), 7)
    stream_in = scatter_about(key_of[0], (MICRO, TOKENS, D), 1.0, 6.0, ((0, 2), (1, 8)))
    queries = draw_queries(jax.random.fold_in(key_of[6], 71), 0)
    keys = draw_keys(jax.random.fold_in(key_of[6], 71), 0)
    values = scatter_about(key_of[3], (MICRO, TOKENS, HEADS * HD), 1.0, 6.0, ((0, 2), (1, 8), (2, 2)))
    out_weight = scatter_about(key_of[4], (MICRO, HEADS * HD, D), (HEADS * HD) ** -0.5, 0.15625, ((0, 2), (1, 2)))
    gate_scale = jnp.clip(jnp.exp(math.log(2.0) - 1.3862944 * jax.random.uniform(key_of[5], (MICRO, D), jnp.float32) ** steps_of(key_of[5], (MICRO, D), ((0, 2),), -0.2, 0.2)), 0.5, 2.0)
    return {"stream_in": stream_in, "queries": queries, "keys": keys, "values": values, "out_weight": out_weight, "gate_scale": gate_scale}


def attend_head(operands):
    query_head, key_head, value_head = operands
    scores = jnp.dot(query_head, key_head.T, preferred_element_type=jnp.float32) * (1.0 / math.sqrt(HD))
    peak = lax.optimization_barrier(jnp.max(scores, axis=1, keepdims=True))
    raised = jnp.exp(scores - peak)
    row_total = lax.optimization_barrier(jnp.sum(raised, axis=1, keepdims=True))
    mixed = jnp.dot(raised.astype(jnp.bfloat16), value_head, preferred_element_type=jnp.float32)
    return (mixed / row_total).astype(jnp.bfloat16)

def video_rows(array, video):
    width = array.shape[1]
    return array.reshape(CYCLE, VIDEOS, TOK_DEV, width)[:, video].reshape(SEQ, width)

def attend_video(query_rows, key_rows, value_rows):
    query_heads = query_rows.reshape(SEQ, HEADS, HD).transpose(1, 0, 2)
    key_heads = key_rows.reshape(SEQ, HEADS, HD).transpose(1, 0, 2)
    value_heads = value_rows.reshape(SEQ, HEADS, HD).transpose(1, 0, 2)
    attended = lax.map(attend_head, (query_heads, key_heads, value_heads))
    return attended.transpose(1, 0, 2).reshape(SEQ, HEADS * HD)

def section(stream, query_rows, key_rows, value_rows, weight, gating):
    pieces = [attend_video(video_rows(query_rows, video), video_rows(key_rows, video), video_rows(value_rows, video)) for video in range(VIDEOS)]
    stacked = jnp.stack(pieces).reshape(VIDEOS, CYCLE, TOK_DEV, HEADS * HD)
    attended = stacked.transpose(1, 0, 2, 3).reshape(TOKENS, HEADS * HD)
    branch = jnp.dot(attended, weight, preferred_element_type=jnp.float32)
    return (stream.astype(jnp.float32) + gating[None, :] * branch).astype(jnp.bfloat16)

def reference(stream_in, queries, keys, values, out_weight, gate_scale):
    updated = jnp.stack([section(stream_in[index], queries[index], keys[index], values[index], out_weight[index], gate_scale[index]) for index in range(MICRO)])
    return jnp.roll(updated, 1, axis=0)
```

```python
import functools
import math

import jax
import jax.numpy as jnp
from jax import lax
from jax.experimental import pallas as pl
from jax.experimental.pallas import tpu as pltpu
from jax.sharding import PartitionSpec as P

HD = 128
LOG2E = 1.4426950408889634
VMEM = pl.BlockSpec(memory_space=pltpu.VMEM)


def absorb_kernel(heads, first, last, *refs):
    count = len(heads)
    q_ref = refs[0]
    kv_refs = refs[1 : 1 + count]
    rest = refs[1 + count :]
    if not first:
        top_in, total_in, mixed_in = rest[:3]
        rest = rest[3:]
    factor = LOG2E / math.sqrt(HD)
    for place, head in enumerate(heads):
        query = q_ref[:, head * HD : (head + 1) * HD]
        key = kv_refs[place][:, :HD]
        value = kv_refs[place][:, HD:]
        scores = lax.dot_general(
            query, key, (((1,), (1,)), ((), ())), preferred_element_type=jnp.float32
        )
        top = jnp.max(scores, axis=1, keepdims=True)
        if not first:
            top_old = top_in[place]
            top = jnp.maximum(top_old[:, :1], top)
        raised = jnp.exp2((scores - top) * factor).astype(jnp.bfloat16)
        wide = jnp.concatenate([value, jnp.ones_like(value)], axis=1)
        both = jnp.dot(raised, wide, preferred_element_type=jnp.float32)
        mixed, total = both[:, :HD], both[:, HD:]
        if not first:
            shrink = jnp.exp2((top_old - top) * factor)
            mixed = mixed_in[place] * shrink + mixed
            total = total_in[place] * shrink + total
        if last:
            rest[0][:, place * HD : (place + 1) * HD] = (mixed / total).astype(jnp.bfloat16)
        else:
            rest[0][place] = jnp.broadcast_to(top, mixed.shape)
            rest[1][place] = total
            rest[2][place] = mixed


def absorb(query, blocks, heads, state, last):
    rows = query.shape[0]
    count = len(heads)
    first = state is None
    if last:
        out_shape = jax.ShapeDtypeStruct((rows, count * HD), jnp.bfloat16)
        out_specs = VMEM
    else:
        out_shape = (jax.ShapeDtypeStruct((count, rows, HD), jnp.float32),) * 3
        out_specs = (VMEM,) * 3
    operands = [query, *blocks] + ([] if first else list(state))
    keys = blocks[0].shape[0]
    return pl.pallas_call(
        functools.partial(absorb_kernel, heads, first, last),
        out_shape=out_shape,
        in_specs=[VMEM] * len(operands),
        out_specs=out_specs,
        cost_estimate=pl.CostEstimate(
            flops=4 * count * rows * keys * HD,
            bytes_accessed=count * rows * HD * 12,
            transcendentals=count * rows * keys,
        ),
        name="absorb",
    )(*operands)


def project_kernel(parts, finish, *refs):
    refs = list(refs)
    pieces = [refs.pop(0) for _ in parts]
    weights = {}
    for source, _ in parts:
        if source not in weights:
            weights[source] = refs.pop(0)
    total = None
    if finish:
        total = refs.pop(0)[...]
        stream, gate = refs.pop(0), refs.pop(0)
    for piece, (source, heads) in zip(pieces, parts):
        for place, head in enumerate(heads):
            term = jnp.dot(
                piece[:, place * HD : (place + 1) * HD],
                weights[source][head * HD : (head + 1) * HD, :],
                preferred_element_type=jnp.float32,
            )
            total = term if total is None else total + term
    if finish:
        refs[0][...] = (stream[...].astype(jnp.float32) + gate[...] * total).astype(jnp.bfloat16)
    else:
        refs[0][...] = total


def project(pieces, parts, weights, finishing):
    rows = pieces[0].shape[0]
    cols = next(iter(weights.values())).shape[1]
    used = []
    for source, _ in parts:
        if source not in used:
            used.append(source)
    operands = [*pieces, *[weights[source] for source in used]]
    finish = finishing is not None
    if finish:
        operands += list(finishing)
    depth = sum(len(heads) for _, heads in parts) * HD
    return pl.pallas_call(
        functools.partial(project_kernel, parts, finish),
        out_shape=jax.ShapeDtypeStruct((rows, cols), jnp.bfloat16 if finish else jnp.float32),
        in_specs=[VMEM] * len(operands),
        out_specs=VMEM,
        cost_estimate=pl.CostEstimate(
            flops=2 * rows * depth * cols, bytes_accessed=rows * cols * 4, transcendentals=0
        ),
        name="project",
    )(*operands)


def per_device(stream_in, queries, keys, values, out_weight, gate_scale):
    sections = lax.axis_size("segment")
    seq_count = lax.axis_size("seq")
    shares = lax.axis_size("head")
    heads_dev = queries.shape[2] // HD
    cycle_len = min(32, seq_count)
    stride = seq_count // cycle_len

    ring = list(range(0, cycle_len, 2)) + list(range(1, cycle_len, 2))[::-1]
    after = {ring[at]: ring[(at + 1) % cycle_len] for at in range(cycle_len)}
    before = {target: source for source, target in after.items()}

    def hop(block, towards, shift):
        pairs = []
        for section in range(sections):
            for member in range(cycle_len):
                for video in range(stride):
                    pairs.append(
                        (
                            section * seq_count + member * stride + video,
                            (section + shift) % sections * seq_count
                            + towards[member] * stride
                            + video,
                        )
                    )
        return lax.ppermute(block, ("segment", "seq"), pairs)

    def next_core(block):
        return lax.ppermute(
            block, "segment", [(at, (at + 1) % sections) for at in range(sections)]
        )

    def across(block, by, shift):
        pairs = []
        for section in range(sections):
            for share in range(shares):
                pairs.append(
                    (
                        section * shares + share,
                        (section + shift) % sections * shares + (share + by) % shares,
                    )
                )
        return lax.ppermute(block, ("segment", "head"), pairs)

    def columns(array, head):
        return array[0, :, head * HD : (head + 1) * HD]

    half = heads_dev // 2
    chains = [(at, half + at) for at in range(half)]
    own = {}
    for chain in chains:
        for head in chain:
            own[head] = jnp.concatenate([columns(keys, head), columns(values, head)], axis=1)
    ways = (after, before)

    moving = {chain: [hop(own[head], way, 1) for head, way in zip(chain, ways)] for chain in chains}
    query = next_core(queries[0])
    state = {}
    here = {chain: [next_core(own[head]) for head in chain] for chain in chains}

    share = lax.axis_index("head")
    col_count = out_weight.shape[2] // shares

    def cut(array, by):
        start = lax.rem(share + by, shares) * col_count
        return lax.dynamic_slice_in_dim(array, start, col_count, array.ndim - 1)

    weights = {by: across(cut(out_weight[0], by), by, 1) for by in range(1, shares)}
    weights[0] = next_core(cut(out_weight[0], 0))
    stream = next_core(cut(stream_in[0], 0))
    gate = next_core(cut(gate_scale, 0))

    for chain in chains:
        state[chain] = absorb(query, here[chain], chain, None, False)

    def advance(chain, arrived, held, last):
        arrived, held = lax.optimization_barrier((arrived, held))
        following = None
        if not last:
            following = [hop(block, way, 0) for block, way in zip(arrived, ways)]
        return following, absorb(query, arrived, chain, held, last)

    attended = {}
    if cycle_len <= 8:
        for step in range(1, cycle_len - 1):
            for chain in chains:
                moving[chain], state[chain] = advance(chain, moving[chain], state[chain], False)
    else:

        def turn(_, carry):
            return [advance(chain, *carry[at], False) for at, chain in enumerate(chains)]

        carry = lax.fori_loop(
            1, cycle_len - 1, turn, [(moving[chain], tuple(state[chain])) for chain in chains]
        )
        moving = {chain: carry[at][0] for at, chain in enumerate(chains)}
        state = {chain: carry[at][1] for at, chain in enumerate(chains)}
    for chain in chains:
        attended[chain] = advance(chain, moving[chain], state[chain], True)[1]

    final_pieces, final_parts = [], []
    pieces, parts = [], []
    for at, chain in enumerate(chains):
        pieces.append(attended[chain])
        parts.append((0, chain))
        for by in range(1, shares):
            other = across(attended[chain], by, 0)
            if at == len(chains) - 1:
                final_pieces.append(other)
                final_parts.append((by, chain))
            else:
                pieces.append(other)
                parts.append((by, chain))
    total = project(pieces, tuple(parts), weights, None)
    out = project(final_pieces, tuple(final_parts), weights, (total, stream, gate))
    return out[None]


def solution(mesh):
    return jax.shard_map(
        per_device,
        mesh=mesh,
        in_specs=(
            P("segment", "seq", None),
            P("segment", "seq", "head"),
            P("segment", "seq", "head"),
            P("segment", "seq", "head"),
            P("segment", "head", None),
            P("segment", None),
        ),
        out_specs=P("segment", "seq", "head"),
        check_vma=False,
    )
```

```python
import functools
import math

import jax
import jax.numpy as jnp
from jax import lax
from jax.experimental import pallas as pl
from jax.experimental.pallas import tpu as pltpu
from jax.sharding import PartitionSpec as P


HD = 128
STATE = HD + 16
UNROLL = 8
LOG2E = 1.4426950408889634
VMEM = pl.BlockSpec(memory_space=pltpu.VMEM)


def limit(mib):
    return pltpu.CompilerParams(vmem_limit_bytes=mib << 20)


def pack_kernel(groups, k_ref, v_ref, *out_refs):
    rows = k_ref.shape[0]
    for heads, out in zip(groups, out_refs):
        for place, head in enumerate(heads):
            lanes = slice(head * HD, (head + 1) * HD)
            base = place * 2 * HD
            for piece in range(rows // HD):
                out[base : base + HD, piece * HD : (piece + 1) * HD] = k_ref[
                    piece * HD : (piece + 1) * HD, lanes
                ]
            out[base + HD : base + 2 * HD, :] = v_ref[:, lanes].T


def pack(keys, values, groups):
    rows = keys.shape[0]
    return pl.pallas_call(
        functools.partial(pack_kernel, groups),
        out_shape=tuple(
            jax.ShapeDtypeStruct((len(heads) * 2 * HD, rows), jnp.bfloat16) for heads in groups
        ),
        in_specs=[VMEM] * 2,
        out_specs=(VMEM,) * len(groups),
        compiler_params=limit(8),
        name="pack",
    )(keys, values)


def turn_kernel(x_ref, out_ref):
    for head in range(x_ref.shape[1] // HD):
        lanes = slice(head * HD, (head + 1) * HD)
        out_ref[lanes, :] = x_ref[:, lanes].T


def turned(x):
    return pl.pallas_call(
        turn_kernel,
        out_shape=jax.ShapeDtypeStruct((x.shape[1], x.shape[0]), x.dtype),
        in_specs=[VMEM],
        out_specs=VMEM,
        compiler_params=limit(8),
        name="turned",
    )(x)


def absorb_kernel(groups, first, last, *refs):
    q_ref = refs[0]
    kv_refs = refs[1 : 1 + len(groups)]
    out = refs[-1]
    state = None if first else refs[-2]
    keys = kv_refs[0].shape[1]
    factor = LOG2E / math.sqrt(HD)
    at = 0
    for kv, heads in zip(kv_refs, groups):
        for place, head in enumerate(heads):
            base = place * 2 * HD
            query = q_ref[head * HD : (head + 1) * HD, :]
            key = jnp.concatenate(
                [
                    kv[base : base + HD, piece * HD : (piece + 1) * HD]
                    for piece in range(keys // HD)
                ],
                axis=0,
            )
            scores = jnp.dot(key, query, preferred_element_type=jnp.float32)
            top = jnp.max(scores, axis=0, keepdims=True)
            if not first:
                top_old = state[at, HD + 8 : HD + 9, :]
                top = jnp.maximum(top_old, top)
            raised = jnp.exp2((scores - top) * factor).astype(jnp.bfloat16)
            value = kv[base + HD : base + 2 * HD, :]
            tall = jnp.concatenate([value, jnp.ones((16, keys), jnp.bfloat16)], axis=0)
            both = jnp.dot(tall, raised, preferred_element_type=jnp.float32)
            mixed, total = both[:HD], both[HD : HD + 8]
            if not first:
                shrink = jnp.exp2((top_old - top) * factor)
                mixed = state[at, :HD, :] * shrink + mixed
                total = state[at, HD : HD + 8, :] * shrink + total
            if last:
                done = mixed / total[:1]
                out[:, at * HD : (at + 1) * HD] = done.T.astype(jnp.bfloat16)
            else:
                out[at, :HD, :] = mixed
                out[at, HD : HD + 8, :] = total
                out[at, HD + 8 :, :] = jnp.broadcast_to(top, total.shape)
            at += 1


def absorb(query, blocks, groups, state, last):
    rows = query.shape[1]
    keys = blocks[0].shape[1]
    count = sum(len(heads) for heads in groups)
    first = state is None
    if last:
        out_shape = jax.ShapeDtypeStruct((rows, count * HD), jnp.bfloat16)
    else:
        out_shape = jax.ShapeDtypeStruct((count, STATE, rows), jnp.float32)
    operands = [query, *blocks] + ([] if first else [state])
    return pl.pallas_call(
        functools.partial(absorb_kernel, groups, first, last),
        out_shape=out_shape,
        in_specs=[VMEM] * len(operands),
        out_specs=VMEM,
        input_output_aliases={} if first or last else {len(operands) - 1: 0},
        cost_estimate=pl.CostEstimate(
            flops=4 * count * rows * keys * HD,
            bytes_accessed=count * rows * HD * 12,
            transcendentals=count * rows * keys,
        ),
        compiler_params=limit(8),
        name="absorb",
    )(*operands)


def main_kernel(plan, *refs):
    out = refs[-1]
    refs = list(refs[1:-1])
    total = None
    for layout in plan:
        pieces = [refs.pop(0) for _ in layout]
        weight = refs.pop(0)
        slots = {}
        for piece, heads in zip(pieces, layout):
            for place, head in enumerate(heads):
                slots[head] = piece[:, place * HD : (place + 1) * HD]
        order = sorted(slots)
        left = jnp.concatenate([slots[head] for head in order], axis=1)
        if len(order) * HD == weight.shape[0]:
            right = weight[...]
        else:
            right = jnp.concatenate(
                [weight[head * HD : (head + 1) * HD, :] for head in order], axis=0
            )
        term = jnp.dot(left, right, preferred_element_type=jnp.float32)
        total = term if total is None else total + term
    out[...] = total


def project_main(share, sources, wide):
    rows = sources[0][0][0].shape[0]
    cols = [s[2].shape[1] for s in sources if not s[3]]
    cols = cols[0] if cols else sources[0][2].shape[1]
    steps = cols // wide
    operands, specs, plan = [], [], []
    for pieces, layout, weight, whole in sources:
        for piece in pieces:
            operands.append(piece)
            specs.append(pl.BlockSpec(piece.shape, lambda j, s: (0, 0)))
        operands.append(weight)
        specs.append(
            pl.BlockSpec(
                (weight.shape[0], wide),
                (lambda j, s: (0, s[0] * steps + j)) if whole else (lambda j, s: (0, j)),
            )
        )
        plan.append(layout)
    return pl.pallas_call(
        functools.partial(main_kernel, plan),
        out_shape=jax.ShapeDtypeStruct((rows, cols), jnp.float32),
        grid_spec=pltpu.PrefetchScalarGridSpec(
            num_scalar_prefetch=1,
            grid=(steps,),
            in_specs=specs,
            out_specs=pl.BlockSpec((rows, wide), lambda j, s: (0, j)),
        ),
        cost_estimate=pl.CostEstimate(
            flops=4 * rows * 768 * cols, bytes_accessed=rows * cols * 4, transcendentals=0
        ),
        compiler_params=limit(12),
        name="project_main",
    )(share, *operands)


def last_kernel(counts, *refs):
    out, gate, stream, total = refs[-1], refs[-2], refs[-3], refs[-4]
    refs = list(refs[1:-4])
    branch = total[...]
    for count in counts:
        piece = refs.pop(0)
        right = jnp.concatenate([refs.pop(0)[...] for _ in range(count)], axis=0)
        branch = branch + jnp.dot(piece[...], right, preferred_element_type=jnp.float32)
    out[...] = (stream[...].astype(jnp.float32) + gate[...] * branch).astype(jnp.bfloat16)


def project_last(share, late, total, stream, gate, wide):
    rows, cols = total.shape
    steps = cols // wide
    operands, specs, counts = [], [], []
    for piece, heads, weight in late:
        operands.append(piece)
        specs.append(pl.BlockSpec(piece.shape, lambda j, s: (0, 0)))
        for head in heads:
            operands.append(weight)
            specs.append(pl.BlockSpec((HD, wide), lambda j, s, head=head: (head, j)))
        counts.append(len(heads))
    operands += [total, stream, gate]
    specs += [
        pl.BlockSpec((rows, wide), lambda j, s: (0, j)),
        pl.BlockSpec((rows, wide), lambda j, s: (0, s[0] * steps + j)),
        pl.BlockSpec((1, wide), lambda j, s: (0, s[0] * steps + j)),
    ]
    return pl.pallas_call(
        functools.partial(last_kernel, counts),
        out_shape=jax.ShapeDtypeStruct((rows, cols), jnp.bfloat16),
        grid_spec=pltpu.PrefetchScalarGridSpec(
            num_scalar_prefetch=1,
            grid=(steps,),
            in_specs=specs,
            out_specs=pl.BlockSpec((rows, wide), lambda j, s: (0, j)),
        ),
        cost_estimate=pl.CostEstimate(
            flops=2 * rows * 256 * cols, bytes_accessed=rows * cols * 8, transcendentals=0
        ),
        compiler_params=limit(12),
        name="project_last",
    )(share, *operands)


def per_device(stream_in, queries, keys, values, out_weight, gate_scale):
    sections = lax.axis_size("segment")
    seq_count = lax.axis_size("seq")
    shares = lax.axis_size("head")
    heads_dev = queries.shape[2] // HD
    cycle_len = min(32, seq_count)
    stride = seq_count // cycle_len

    ring = list(range(0, cycle_len, 2)) + list(range(1, cycle_len, 2))[::-1]
    after = {ring[at]: ring[(at + 1) % cycle_len] for at in range(cycle_len)}
    before = {target: source for source, target in after.items()}
    ways = (after, before)

    def hop(block, towards, shift):
        pairs = []
        for section in range(sections):
            for member in range(cycle_len):
                for video in range(stride):
                    pairs.append(
                        (
                            section * seq_count + member * stride + video,
                            (section + shift) % sections * seq_count
                            + towards[member] * stride
                            + video,
                        )
                    )
        return lax.ppermute(block, ("segment", "seq"), pairs)

    def next_core(block):
        return lax.ppermute(
            block, "segment", [(at, (at + 1) % sections) for at in range(sections)]
        )

    def across(block, by, shift):
        pairs = []
        for section in range(sections):
            for share in range(shares):
                pairs.append(
                    (
                        section * shares + share,
                        (section + shift) % sections * shares + (share + by) % shares,
                    )
                )
        return lax.ppermute(block, ("segment", "head"), pairs)

    half = heads_dev // 2
    early = half - max(1, half // 3)
    cuts = [(0, early), (early, half)] if early else [(0, half)]
    chains = [(tuple(range(a, b)), tuple(range(half + a, half + b))) for a, b in cuts]

    packed = pack(keys[0], values[0], [heads for chain in chains for heads in chain])
    own = [packed[2 * at : 2 * at + 2] for at in range(len(chains))]
    moving = []
    for at in range(len(chains)):
        moving.append([])
        for side, block in enumerate(own[at]):
            moving[at].append(hop(block, ways[side], 1))
    query = next_core(turned(queries[0]))
    here = [[next_core(block) for block in own[at]] for at in range(len(chains))]

    share = lax.axis_index("head")
    col_count = out_weight.shape[2] // shares
    weights = {}
    for by in range(1, shares):
        start = lax.rem(share + by, shares) * col_count
        part = lax.dynamic_slice_in_dim(out_weight[0], start, col_count, 1)
        weights[by] = across(part, by, 1)
    weights[0] = next_core(out_weight[0])
    stream = next_core(stream_in[0])
    gate = next_core(gate_scale)

    def fold(at, arrived, held, last):
        return absorb(query, arrived, chains[at], held, last)

    def send(arrived):
        sent = []
        for side, block in enumerate(arrived):
            sent.append(hop(block, ways[side], 0))
        return sent

    everyone = range(len(chains))
    state = [fold(at, here[at], None, False) for at in everyone]
    if cycle_len <= UNROLL:
        for _ in range(1, cycle_len - 1):
            for at in everyone:
                arrived = moving[at]
                moving[at] = send(arrived)
                state[at] = fold(at, arrived, state[at], False)
    else:

        def turn(_, carry):
            moving, state = carry
            onward = [send(moving[at]) for at in everyone]
            return onward, [fold(at, moving[at], state[at], False) for at in everyone]

        moving, state = lax.fori_loop(1, cycle_len - 1, turn, (moving, state))
    attended = [fold(at, moving[at], state[at], True) for at in everyone]
    others = []
    for at in range(len(chains)):
        others.append([across(attended[at], by, 0) for by in range(1, shares)])

    flat = [first + second for first, second in chains]
    sources = [(attended, flat, weights[0], True)]
    if len(chains) > 1:
        for by in range(1, shares):
            sources.append(([other[by - 1] for other in others[:-1]], flat[:-1], weights[by], False))
    share_ref = share.astype(jnp.int32).reshape(1)
    total = project_main(share_ref, sources, 512)
    late = [(others[-1][by - 1], flat[-1], weights[by]) for by in range(1, shares)]
    return project_last(share_ref, late, total, stream, gate, 512)[None]


def solution(mesh):
    return jax.shard_map(
        per_device,
        mesh=mesh,
        in_specs=(
            P("segment", "seq", None),
            P("segment", "seq", "head"),
            P("segment", "seq", "head"),
            P("segment", "seq", "head"),
            P("segment", "head", None),
            P("segment", None),
        ),
        out_specs=P("segment", "seq", "head"),
        check_vma=False,
    )
```

```python
import functools
import math

import jax
import jax.numpy as jnp
from jax import lax
from jax.experimental import pallas as pl
from jax.experimental.pallas import tpu as pltpu
from jax.sharding import PartitionSpec as P


HD = 128
STATE = HD + 16
LOG2E = 1.4426950408889634
VMEM = pl.BlockSpec(memory_space=pltpu.VMEM)


def limit(mib):
    return pltpu.CompilerParams(vmem_limit_bytes=mib << 20)


def pack_kernel(groups, role_ref, k_ref, v_ref, *out_refs):
    rows, width = k_ref.shape
    half = width // 2
    for side in range(2):
        role = role_ref[0] if side == 0 else 1 - role_ref[0]
        for heads, out in zip(groups, out_refs[side * len(groups) :]):
            for place, head in enumerate(heads):
                lanes = pl.ds(pl.multiple_of(role * half + head * HD, HD), HD)
                base = place * 2 * HD
                for piece in range(rows // HD):
                    out[base : base + HD, piece * HD : (piece + 1) * HD] = k_ref[
                        piece * HD : (piece + 1) * HD, lanes
                    ]
                out[base + HD : base + 2 * HD, :] = v_ref[:, lanes].T


SMEM = pl.BlockSpec(memory_space=pltpu.SMEM)


def pack(role, keys, values, groups):
    rows = keys.shape[0]
    shapes = [jax.ShapeDtypeStruct((len(heads) * 2 * HD, rows), jnp.bfloat16) for heads in groups]
    return pl.pallas_call(
        functools.partial(pack_kernel, groups),
        out_shape=tuple(shapes + shapes),
        in_specs=[SMEM, VMEM, VMEM],
        out_specs=(VMEM,) * (2 * len(groups)),
        compiler_params=limit(8),
        name="pack",
    )(role, keys, values)


def turn_kernel(role_ref, x_ref, mine_ref, give_ref):
    half = x_ref.shape[1] // 2
    for out, role in ((mine_ref, role_ref[0]), (give_ref, 1 - role_ref[0])):
        for head in range(half // HD):
            lanes = pl.ds(pl.multiple_of(role * half + head * HD, HD), HD)
            out[head * HD : (head + 1) * HD, :] = x_ref[:, lanes].T


def turned(role, x):
    shape = jax.ShapeDtypeStruct((x.shape[1] // 2, x.shape[0]), x.dtype)
    return pl.pallas_call(
        turn_kernel,
        out_shape=(shape, shape),
        in_specs=[SMEM, VMEM],
        out_specs=(VMEM, VMEM),
        compiler_params=limit(8),
        name="turned",
    )(role, x)


def absorb_kernel(heads, count, first, last, *refs):
    q_refs, kv_refs, rest = refs[:2], refs[2 : 2 + count], refs[2 + count :]
    state = None if first else rest[0]
    outs = rest if first else rest[1:]
    keys = kv_refs[0].shape[1]
    factor = LOG2E / math.sqrt(HD)
    for place, head in enumerate(heads):
        base = place * 2 * HD
        key = jnp.concatenate(
            [
                kv[base : base + HD, piece * HD : (piece + 1) * HD]
                for kv in kv_refs
                for piece in range(keys // HD)
            ],
            axis=0,
        )
        value = jnp.concatenate([kv[base + HD : base + 2 * HD, :] for kv in kv_refs], axis=1)
        tall = jnp.concatenate([value, jnp.ones((16, value.shape[1]), jnp.bfloat16)], axis=0)
        for side, q_ref in enumerate(q_refs):
            query = q_ref[head * HD : (head + 1) * HD, :]
            scores = jnp.dot(key, query, preferred_element_type=jnp.float32)
            top = jnp.max(scores, axis=0, keepdims=True)
            if not first:
                top_old = state[place, side, HD + 8 : HD + 9, :]
                top = jnp.maximum(top_old, top)
            raised = jnp.exp2((scores - top) * factor).astype(jnp.bfloat16)
            both = jnp.dot(tall, raised, preferred_element_type=jnp.float32)
            mixed, total = both[:HD], both[HD : HD + 8]
            if not first:
                shrink = jnp.exp2((top_old - top) * factor)
                mixed = state[place, side, :HD, :] * shrink + mixed
                total = state[place, side, HD : HD + 8, :] * shrink + total
            if last:
                done = mixed / total[:1]
                outs[side][:, place * HD : (place + 1) * HD] = done.T.astype(jnp.bfloat16)
            else:
                outs[0][place, side, :HD, :] = mixed
                outs[0][place, side, HD : HD + 8, :] = total
                outs[0][place, side, HD + 8 :, :] = jnp.broadcast_to(top, total.shape)


def absorb(asking, blocks, heads, state, last):
    rows = asking[0].shape[1]
    keys = blocks[0].shape[1] * len(blocks)
    count = len(heads)
    first = state is None
    if last:
        shape = jax.ShapeDtypeStruct((rows, count * HD), jnp.bfloat16)
        out_shape, out_specs = (shape, shape), (VMEM, VMEM)
    else:
        out_shape = jax.ShapeDtypeStruct((count, 2, STATE, rows), jnp.float32)
        out_specs = VMEM
    operands = [*asking, *blocks] + ([] if first else [state])
    return pl.pallas_call(
        functools.partial(absorb_kernel, heads, len(blocks), first, last),
        out_shape=out_shape,
        in_specs=[VMEM] * len(operands),
        out_specs=out_specs,
        input_output_aliases={} if first or last else {len(operands) - 1: 0},
        cost_estimate=pl.CostEstimate(
            flops=8 * count * rows * keys * HD,
            bytes_accessed=count * rows * HD * 12,
            transcendentals=2 * count * rows * keys,
        ),
        compiler_params=limit(12),
        name="absorb",
    )(*operands)


def project_kernel(uses, finish, *refs):
    out = refs[-1]
    refs = list(refs[1:-1])
    total = None
    if finish:
        total = refs[-3][...]
    for weight_count, pieces in uses:
        lefts = [refs.pop(0)[...] for _ in range(pieces)]
        rights = [refs.pop(0)[...] for _ in range(weight_count)]
        left = lefts[0] if pieces == 1 else jnp.concatenate(lefts, axis=1)
        right = rights[0] if weight_count == 1 else jnp.concatenate(rights, axis=0)
        term = jnp.dot(left, right, preferred_element_type=jnp.float32)
        total = term if total is None else total + term
    if finish:
        stream, gate = refs[-2], refs[-1]
        total = stream[...].astype(jnp.float32) + gate[...] * total
    out[...] = total.astype(out.dtype)


def project(where, sources, cols, wide, finishing=None):
    rows = sources[0][0][0].shape[0]
    steps = cols // wide
    operands, specs, uses = [], [], []
    for pieces, weight, whole, flip, heads in sources:
        for piece in pieces:
            operands.append(piece)
            specs.append(pl.BlockSpec(piece.shape, lambda j, s: (0, 0)))
        per_role = weight.shape[0] // HD // 2

        def place(j, s, head, whole=whole, flip=flip, per_role=per_role, unit=HD):
            role = 1 - s[1] if flip else s[1]
            at = role if unit != HD else role * per_role + head
            return at, (s[0] * steps + j if whole else j)

        if tuple(heads) == tuple(range(per_role)):
            operands.append(weight)
            specs.append(
                pl.BlockSpec(
                    (per_role * HD, wide), functools.partial(place, head=0, unit=per_role * HD)
                )
            )
            uses.append((1, len(pieces)))
        else:
            for head in heads:
                operands.append(weight)
                specs.append(pl.BlockSpec((HD, wide), functools.partial(place, head=head)))
            uses.append((len(heads), len(pieces)))
    if finishing is not None:
        operands += list(finishing)
        specs += [
            pl.BlockSpec((rows, wide), lambda j, s: (0, j)),
            pl.BlockSpec((rows, wide), lambda j, s: (0, s[0] * steps + j)),
            pl.BlockSpec((1, wide), lambda j, s: (0, s[0] * steps + j)),
        ]
    depth = sum(len(source[4]) for source in sources) * HD
    return pl.pallas_call(
        functools.partial(project_kernel, uses, finishing is not None),
        out_shape=jax.ShapeDtypeStruct(
            (rows, cols), jnp.float32 if finishing is None else jnp.bfloat16
        ),
        grid_spec=pltpu.PrefetchScalarGridSpec(
            num_scalar_prefetch=1,
            grid=(steps,),
            in_specs=specs,
            out_specs=pl.BlockSpec((rows, wide), lambda j, s: (0, j)),
        ),
        cost_estimate=pl.CostEstimate(
            flops=2 * rows * depth * cols, bytes_accessed=rows * cols * 4, transcendentals=0
        ),
        compiler_params=limit(12),
        name="project",
    )(where, *operands)


def role_of(member):
    return (member // 2 + 1) // 2 % 2


def per_device(stream_in, queries, keys, values, out_weight, gate_scale):
    sections = lax.axis_size("segment")
    seq_count = lax.axis_size("seq")
    shares = lax.axis_size("head")
    local = queries.shape[2] // HD // 2
    cycle_len = min(32, seq_count)
    stride = seq_count // cycle_len
    planes = cycle_len // 2
    rounds = planes // 2

    partner = {m: m ^ 2 for m in range(cycle_len)}
    beside = {m: m ^ 1 for m in range(cycle_len)}
    beyond = {}
    for role in range(2):
        for column in range(2):
            line = [p * 2 + column for p in range(planes) if role_of(p * 2) == role]
            for at, m in enumerate(line):
                beyond[m] = line[(at + 1) % len(line)]

    def hop(block, towards, shift=0, by=0):
        pairs = []
        for section in range(sections):
            for member in range(cycle_len):
                for video in range(stride):
                    for share in range(shares):
                        origin = section * seq_count + member * stride + video
                        target = (
                            (section + shift) % sections * seq_count
                            + towards[member] * stride
                            + video
                        )
                        pairs.append(
                            (origin * shares + share, target * shares + (share + by) % shares)
                        )
        return lax.ppermute(block, ("segment", "seq", "head"), pairs)

    still = {m: m for m in range(cycle_len)}
    share = lax.axis_index("head").astype(jnp.int32)
    role = role_of(lax.axis_index("seq").astype(jnp.int32) // stride)
    role_ref = role.reshape(1)
    where = jnp.stack([share, role])

    early = local - max(1, local // 3)
    groups = [tuple(range(early)), tuple(range(early, local))] if early else [tuple(range(local))]
    everyone = range(len(groups))

    packed = pack(role_ref, keys[0], values[0], groups)
    mine, give = packed[: len(groups)], packed[len(groups) :]
    my_query, give_query = turned(role_ref, queries[0])
    got = [None] * len(groups)
    far = [[None] * 2 for _ in groups]
    near = [[None] * 2 for _ in groups]
    own = [None] * len(groups)
    for g in everyone:
        got[g] = hop(give[g], partner, 1)
        far[g][0] = hop(mine[g], beyond, 1)
        near[g][0] = hop(mine[g], beside, 1)
        own[g] = hop(mine[g], still, 1)
    asking = [hop(my_query, still, 1), hop(give_query, partner, 1)]

    col_count = out_weight.shape[2] // shares
    weights = {}
    for by in range(1, shares):
        start = lax.rem(share + by, shares) * col_count
        part = lax.dynamic_slice_in_dim(out_weight[0], start, col_count, 1)
        weights[by] = hop(part, still, 1, by)
    weights[0] = hop(out_weight[0], still, 1)
    stream = hop(stream_in[0], still, 1)
    gate = hop(gate_scale, still, 1)

    def fold(g, blocks, held, last=False):
        return absorb(asking, blocks, groups[g], held, last)

    attended = []
    for g in everyone:
        far[g][1] = hop(got[g], beyond)
        near[g][1] = hop(got[g], beside)
        state = fold(g, [own[g], got[g]], None)
        state = fold(g, near[g], state)
        arrived = far[g]
        for turn in range(1, rounds):
            onward = [hop(arrived[i], beside) for i in range(2)]
            following = None
            if turn < rounds - 1:
                following = [hop(arrived[i], beyond) for i in range(2)]
            state = fold(g, arrived, state)
            if turn < rounds - 1:
                state = fold(g, onward, state)
            elif g < len(groups) - 1:
                attended.append(fold(g, onward, state, True))
            else:
                state = fold(g, onward[:1], state)
                attended.append(fold(g, onward[1:], state, True))
            arrived = following

    sources, late = [], []
    for g in everyone:
        ours, theirs = attended[g]
        back = hop(theirs, partner)
        pieces = [(ours, 0, False), (back, 0, True)]
        for by in range(1, shares):
            pieces.append((hop(ours, still, 0, by), by, False))
            pieces.append((hop(theirs, partner, 0, by), by, True))
        for piece, by, flip in pieces:
            source = ([piece], weights[by], by == 0, flip, groups[g])
            if g == len(groups) - 1 and (by or flip):
                late.append(source)
            else:
                sources.append(source)
    if len(groups) > 1:
        mergeable = [source for source in sources if source[2] and not source[3]]
        sources = [source for source in sources if not (source[2] and not source[3])]
        merged = [source[0][0] for source in mergeable]
        sources.append((merged, weights[0], True, False, sum((s[4] for s in mergeable), ())))
    total = project(where, sources, col_count, 512)
    return project(where, late, col_count, 512, (total, stream, gate))[None]


def solution(mesh):
    return jax.shard_map(
        per_device,
        mesh=mesh,
        in_specs=(
            P("segment", "seq", None),
            P("segment", "seq", "head"),
            P("segment", "seq", "head"),
            P("segment", "seq", "head"),
            P("segment", "head", None),
            P("segment", None),
        ),
        out_specs=P("segment", "seq", "head"),
        check_vma=False,
    )
```

```python
import functools
import math

import jax
import jax.numpy as jnp
from jax import lax
from jax.experimental import pallas as pl
from jax.experimental.pallas import tpu as pltpu
from jax.sharding import PartitionSpec as P


HD = 128
STATE = HD + 16
LOG2E = 1.4426950408889634
VMEM = pl.BlockSpec(memory_space=pltpu.VMEM)


def limit(mib):
    return pltpu.CompilerParams(vmem_limit_bytes=mib << 20)


def pack_kernel(groups, role_ref, k_ref, v_ref, *out_refs):
    rows, width = k_ref.shape
    half = width // 2
    for side in range(2):
        role = role_ref[0] if side == 0 else 1 - role_ref[0]
        for heads, out in zip(groups, out_refs[side * len(groups) :]):
            for place, head in enumerate(heads):
                lanes = pl.ds(pl.multiple_of(role * half + head * HD, HD), HD)
                base = place * 2 * HD
                for piece in range(rows // HD):
                    out[base : base + HD, piece * HD : (piece + 1) * HD] = k_ref[
                        piece * HD : (piece + 1) * HD, lanes
                    ]
                out[base + HD : base + 2 * HD, :] = v_ref[:, lanes].T


SMEM = pl.BlockSpec(memory_space=pltpu.SMEM)


def pack(role, keys, values, groups):
    rows = keys.shape[0]
    shapes = [jax.ShapeDtypeStruct((len(heads) * 2 * HD, rows), jnp.bfloat16) for heads in groups]
    return pl.pallas_call(
        functools.partial(pack_kernel, groups),
        out_shape=tuple(shapes + shapes),
        in_specs=[SMEM, VMEM, VMEM],
        out_specs=(VMEM,) * (2 * len(groups)),
        compiler_params=limit(8),
        name="pack",
    )(role, keys, values)


def turn_kernel(role_ref, x_ref, mine_ref, give_ref):
    half = x_ref.shape[1] // 2
    for out, role in ((mine_ref, role_ref[0]), (give_ref, 1 - role_ref[0])):
        for head in range(half // HD):
            lanes = pl.ds(pl.multiple_of(role * half + head * HD, HD), HD)
            out[head * HD : (head + 1) * HD, :] = x_ref[:, lanes].T


def turned(role, x):
    shape = jax.ShapeDtypeStruct((x.shape[1] // 2, x.shape[0]), x.dtype)
    return pl.pallas_call(
        turn_kernel,
        out_shape=(shape, shape),
        in_specs=[SMEM, VMEM],
        out_specs=(VMEM, VMEM),
        compiler_params=limit(8),
        name="turned",
    )(role, x)


def absorb_kernel(heads, count, first, last, *refs):
    q_refs, kv_refs, rest = refs[:2], refs[2 : 2 + count], refs[2 + count :]
    state = None if first else rest[0]
    outs = rest if first else rest[1:]
    keys = kv_refs[0].shape[1]
    factor = LOG2E / math.sqrt(HD)
    for place, head in enumerate(heads):
        base = place * 2 * HD
        key = jnp.concatenate(
            [
                kv[base : base + HD, piece * HD : (piece + 1) * HD]
                for kv in kv_refs
                for piece in range(keys // HD)
            ],
            axis=0,
        )
        value = jnp.concatenate([kv[base + HD : base + 2 * HD, :] for kv in kv_refs], axis=1)
        tall = jnp.concatenate([value, jnp.ones((16, value.shape[1]), jnp.bfloat16)], axis=0)
        for side, q_ref in enumerate(q_refs):
            query = q_ref[head * HD : (head + 1) * HD, :]
            scores = jnp.dot(key, query, preferred_element_type=jnp.float32)
            top = jnp.max(scores, axis=0, keepdims=True)
            if not first:
                top_old = state[place, side, HD + 8 : HD + 9, :]
                top = jnp.maximum(top_old, top)
            raised = jnp.exp2((scores - top) * factor).astype(jnp.bfloat16)
            both = jnp.dot(tall, raised, preferred_element_type=jnp.float32)
            mixed, total = both[:HD], both[HD : HD + 8]
            if not first:
                shrink = jnp.exp2((top_old - top) * factor)
                mixed = state[place, side, :HD, :] * shrink + mixed
                total = state[place, side, HD : HD + 8, :] * shrink + total
            if last:
                done = mixed / total[:1]
                outs[side][:, place * HD : (place + 1) * HD] = done.T.astype(jnp.bfloat16)
            else:
                outs[0][place, side, :HD, :] = mixed
                outs[0][place, side, HD : HD + 8, :] = total
                outs[0][place, side, HD + 8 :, :] = jnp.broadcast_to(top, total.shape)


def absorb(asking, blocks, heads, state, last):
    rows = asking[0].shape[1]
    keys = blocks[0].shape[1] * len(blocks)
    count = len(heads)
    first = state is None
    if last:
        shape = jax.ShapeDtypeStruct((rows, count * HD), jnp.bfloat16)
        out_shape, out_specs = (shape, shape), (VMEM, VMEM)
    else:
        out_shape = jax.ShapeDtypeStruct((count, 2, STATE, rows), jnp.float32)
        out_specs = VMEM
    operands = [*asking, *blocks] + ([] if first else [state])
    return pl.pallas_call(
        functools.partial(absorb_kernel, heads, len(blocks), first, last),
        out_shape=out_shape,
        in_specs=[VMEM] * len(operands),
        out_specs=out_specs,
        input_output_aliases={} if first or last else {len(operands) - 1: 0},
        cost_estimate=pl.CostEstimate(
            flops=8 * count * rows * keys * HD,
            bytes_accessed=count * rows * HD * 12,
            transcendentals=2 * count * rows * keys,
        ),
        compiler_params=limit(12),
        name="absorb",
    )(*operands)


def project_kernel(pieces, *refs):
    out = refs[-1]
    refs = refs[1:-1]
    total = None
    for at in range(pieces):
        term = jnp.dot(
            refs[2 * at][...], refs[2 * at + 1][...], preferred_element_type=jnp.float32
        )
        total = term if total is None else total + term
    base, gate = refs[-2], refs[-1]
    out[...] = (base[...].astype(jnp.float32) + gate[...] * total).astype(out.dtype)


def project(where, sources, base, gate, cols, wide, dtype):
    rows = base.shape[0]
    steps = cols // wide
    operands, specs, depth = [], [], 0
    for piece, lane, weight, row, whole in sources:
        width = piece.shape[1] if lane is None else HD
        depth += width

        def left(j, s, lane=lane):
            return 0, (0 if lane is None else lane(s))

        def right(j, s, row=row, whole=whole):
            return row(s), (s[0] * steps + j if whole else j)

        operands += [piece, weight]
        specs += [pl.BlockSpec((rows, width), left), pl.BlockSpec((width, wide), right)]
    whole = base.shape[1] != cols
    operands += [base, gate]
    specs += [
        pl.BlockSpec((rows, wide), lambda j, s: (0, s[0] * steps + j if whole else j)),
        pl.BlockSpec((1, wide), lambda j, s: (0, s[0] * steps + j)),
    ]
    return pl.pallas_call(
        functools.partial(project_kernel, len(sources)),
        out_shape=jax.ShapeDtypeStruct((rows, cols), dtype),
        grid_spec=pltpu.PrefetchScalarGridSpec(
            num_scalar_prefetch=1,
            grid=(steps,),
            in_specs=specs,
            out_specs=pl.BlockSpec((rows, wide), lambda j, s: (0, j)),
        ),
        cost_estimate=pl.CostEstimate(
            flops=2 * rows * depth * cols, bytes_accessed=rows * cols * 4, transcendentals=0
        ),
        compiler_params=limit(12),
        name="project",
    )(where, *operands)


def role_of(member):
    return (member // 2 + 1) // 2 % 2


def per_device(stream_in, queries, keys, values, out_weight, gate_scale):
    sections = lax.axis_size("segment")
    seq_count = lax.axis_size("seq")
    shares = lax.axis_size("head")
    local = queries.shape[2] // HD // 2
    cycle_len = min(32, seq_count)
    stride = seq_count // cycle_len
    planes = cycle_len // 2
    rounds = planes // 2

    partner = {m: m ^ 2 for m in range(cycle_len)}
    beside = {m: m ^ 1 for m in range(cycle_len)}
    beyond = {}
    for role in range(2):
        for column in range(2):
            line = [p * 2 + column for p in range(planes) if role_of(p * 2) == role]
            for at, m in enumerate(line):
                beyond[m] = line[(at + 1) % len(line)]

    def hop(block, towards, shift=0, by=0):
        pairs = []
        for section in range(sections):
            for member in range(cycle_len):
                for video in range(stride):
                    for share in range(shares):
                        origin = section * seq_count + member * stride + video
                        target = (
                            (section + shift) % sections * seq_count
                            + towards[member] * stride
                            + video
                        )
                        pairs.append(
                            (origin * shares + share, target * shares + (share + by) % shares)
                        )
        return lax.ppermute(block, ("segment", "seq", "head"), pairs)

    still = {m: m for m in range(cycle_len)}
    share = lax.axis_index("head").astype(jnp.int32)
    role = role_of(lax.axis_index("seq").astype(jnp.int32) // stride)
    role_ref = role.reshape(1)
    column = lax.axis_index("seq").astype(jnp.int32) // stride % 2
    where = jnp.stack([share, role, column])
    groups = [(0, 1), (2,)]
    everyone = range(len(groups))

    col_count = out_weight.shape[2] // shares
    lent = {}
    for by in range(1, shares):
        start = lax.rem(share + by, shares) * col_count

        def rows_at(head, count):
            return lax.dynamic_slice(
                out_weight[0], (head * HD, start), (count * HD, col_count)
            )

        lent[by] = [
            hop(rows_at(role * local + 1 - column, 1), still, 1, by),
            hop(rows_at(role * local + 2, 1), still, 1, by),
            hop(rows_at((1 - role) * local, 2), still, 1, by),
        ]

    packed = pack(role_ref, keys[0], values[0], groups)
    mine, give = packed[: len(groups)], packed[len(groups) :]
    my_query, give_query = turned(role_ref, queries[0])
    got = [None] * len(groups)
    far = [[None] * 2 for _ in groups]
    near = [[None] * 2 for _ in groups]
    own = [None] * len(groups)
    everyone = range(len(groups))
    for g in everyone:
        got[g] = hop(give[g], partner, 1)
        far[g][0] = hop(mine[g], beyond, 1)
        near[g][0] = hop(mine[g], beside, 1)
        own[g] = hop(mine[g], still, 1)
    asking = [hop(my_query, still, 1), hop(give_query, partner, 1)]
    weight = hop(out_weight[0], still, 1)
    stream = hop(stream_in[0], still, 1)
    gate = hop(gate_scale, still, 1)
    for by in range(1, shares):
        lent[by].append(hop(lent[by][0], beside))
        lent[by].append(hop(lent[by][1], partner))

    def fold(g, blocks, held, last=False):
        return absorb(asking, blocks, groups[g], held, last)

    attended = []
    for g in everyone:
        far[g][1] = hop(got[g], beyond)
        near[g][1] = hop(got[g], beside)
        state = fold(g, [own[g], got[g]], None)
        state = fold(g, near[g], state)
        arrived = far[g]
        for turn in range(1, rounds):
            onward = [hop(arrived[i], beside) for i in range(2)]
            following = None
            if turn < rounds - 1:
                following = [hop(arrived[i], beyond) for i in range(2)]
            state = fold(g, arrived, state)
            if turn < rounds - 1:
                state = fold(g, onward, state)
            elif g < len(groups) - 1:
                attended.append(fold(g, onward, state, True))
            else:
                state = fold(g, onward[:1], state)
                attended.append(fold(g, onward[1:], state, True))
            arrived = following

    home = []
    for g in everyone:
        ours, theirs = attended[g]
        back = hop(theirs, partner)
        over = {by: hop(ours, still, 0, by) for by in range(1, shares)}
        cross = {by: hop(theirs, partner, 0, by) for by in range(1, shares)}
        home.append((ours, back, over, cross))

    def top(s):
        return 0

    def third(role):
        return role * local + 2

    first, second = home
    sources = []
    for head in range(2):
        pick = lambda s, head=head: head
        sources.append((first[0], pick, weight, lambda s, h=head: s[1] * local + h, True))
        sources.append((first[1], pick, weight, lambda s, h=head: (1 - s[1]) * local + h, True))
    sources.append((second[0], None, weight, lambda s: third(s[1]), True))
    final = [(second[1], None, weight, lambda s: third(1 - s[1]), True)]
    for by in range(1, shares):
        fetched, thirds, pairs, relayed, others = lent[by]
        sources.append((first[2][by], lambda s: 1 - s[2], fetched, top, False))
        sources.append((first[2][by], lambda s: s[2], relayed, top, False))
        sources.append((first[3][by], None, pairs, top, False))
        final.append((second[2][by], None, thirds, top, False))
        final.append((second[3][by], None, others, top, False))
    base = project(where, sources, stream, gate, col_count, 512, jnp.float32)
    return project(where, final, base, gate, col_count, 512, jnp.bfloat16)[None]


def solution(mesh):
    return jax.shard_map(
        per_device,
        mesh=mesh,
        in_specs=(
            P("segment", "seq", None),
            P("segment", "seq", "head"),
            P("segment", "seq", "head"),
            P("segment", "seq", "head"),
            P("segment", "head", None),
            P("segment", None),
        ),
        out_specs=P("segment", "seq", "head"),
        check_vma=False,
    )
```

```python
import functools
import math

import jax
import jax.numpy as jnp
from jax import lax
from jax.experimental import pallas as pl
from jax.experimental.pallas import tpu as pltpu
from jax.sharding import PartitionSpec as P


HD = 128
STATE = HD + 16
LOG2E = 1.4426950408889634
VMEM = pl.BlockSpec(memory_space=pltpu.VMEM)


def limit(mib):
    return pltpu.CompilerParams(vmem_limit_bytes=mib << 20)


def pack_kernel(groups, role_ref, k_any, v_any, *rest):
    out_refs, (k_ref, v_ref, sems) = rest[:-3], rest[-3:]
    loads = [
        pltpu.make_async_copy(k_any, k_ref, sems.at[0]),
        pltpu.make_async_copy(v_any, v_ref, sems.at[1]),
    ]
    for load in loads:
        load.start()
    for load in loads:
        load.wait()
    rows, width = k_ref.shape
    half = width // 2
    for side in range(2):
        role = role_ref[0] if side == 0 else 1 - role_ref[0]
        for heads, out in zip(groups, out_refs[side * len(groups) :]):
            for place, head in enumerate(heads):
                lanes = pl.ds(pl.multiple_of(role * half + head * HD, HD), HD)
                base = place * 2 * HD
                for piece in range(rows // HD):
                    out[base : base + HD, piece * HD : (piece + 1) * HD] = k_ref[
                        piece * HD : (piece + 1) * HD, lanes
                    ]
                out[base + HD : base + 2 * HD, :] = v_ref[:, lanes].T


ANY = pl.BlockSpec(memory_space=pl.ANY)
HBM = pl.BlockSpec(memory_space=pltpu.HBM)
SMEM = pl.BlockSpec(memory_space=pltpu.SMEM)


def in_hbm(x):
    return pltpu.with_memory_space_constraint(x, pltpu.HBM)


def pack(role, keys, values, groups):
    rows = keys.shape[0]
    shapes = [pltpu.VMEM((len(heads) * 2 * HD, rows), jnp.bfloat16) for heads in groups]
    return pl.pallas_call(
        functools.partial(pack_kernel, groups),
        out_shape=tuple(shapes + shapes),
        in_specs=[SMEM, HBM, HBM],
        out_specs=(VMEM,) * (2 * len(groups)),
        scratch_shapes=[
            pltpu.VMEM(keys.shape, keys.dtype),
            pltpu.VMEM(values.shape, values.dtype),
            pltpu.SemaphoreType.DMA((2,)),
        ],
        compiler_params=limit(8),
        name="pack",
    )(role, in_hbm(keys), in_hbm(values))


def turn_kernel(role_ref, x_ref, mine_ref, give_ref):
    half = x_ref.shape[1] // 2
    for out, role in ((mine_ref, role_ref[0]), (give_ref, 1 - role_ref[0])):
        for head in range(half // HD):
            lanes = pl.ds(pl.multiple_of(role * half + head * HD, HD), HD)
            out[head * HD : (head + 1) * HD, :] = x_ref[:, lanes].T


def turned(role, x):
    shape = jax.ShapeDtypeStruct((x.shape[1] // 2, x.shape[0]), x.dtype)
    return pl.pallas_call(
        turn_kernel,
        out_shape=(shape, shape),
        in_specs=[SMEM, VMEM],
        out_specs=(VMEM, VMEM),
        compiler_params=limit(8),
        name="turned",
    )(role, x)


def absorb_kernel(heads, count, first, last, *refs):
    q_refs, kv_refs, rest = refs[:2], refs[2 : 2 + count], refs[2 + count :]
    state = None if first else rest[0]
    outs = rest if first else rest[1:]
    keys = kv_refs[0].shape[1]
    factor = LOG2E / math.sqrt(HD)
    for place, head in enumerate(heads):
        base = place * 2 * HD
        key = jnp.concatenate(
            [
                kv[base : base + HD, piece * HD : (piece + 1) * HD]
                for kv in kv_refs
                for piece in range(keys // HD)
            ],
            axis=0,
        )
        value = jnp.concatenate([kv[base + HD : base + 2 * HD, :] for kv in kv_refs], axis=1)
        tall = jnp.concatenate([value, jnp.ones((16, value.shape[1]), jnp.bfloat16)], axis=0)
        for side, q_ref in enumerate(q_refs):
            query = q_ref[head * HD : (head + 1) * HD, :]
            scores = jnp.dot(key, query, preferred_element_type=jnp.float32)
            top = jnp.max(scores, axis=0, keepdims=True)
            if not first:
                top_old = state[place, side, HD + 8 : HD + 9, :]
                top = jnp.maximum(top_old, top)
            raised = jnp.exp2((scores - top) * factor).astype(jnp.bfloat16)
            both = jnp.dot(tall, raised, preferred_element_type=jnp.float32)
            mixed, total = both[:HD], both[HD : HD + 8]
            if not first:
                shrink = jnp.exp2((top_old - top) * factor)
                mixed = state[place, side, :HD, :] * shrink + mixed
                total = state[place, side, HD : HD + 8, :] * shrink + total
            if last:
                done = mixed / total[:1]
                outs[side][:, place * HD : (place + 1) * HD] = done.T.astype(jnp.bfloat16)
            else:
                outs[0][place, side, :HD, :] = mixed
                outs[0][place, side, HD : HD + 8, :] = total
                outs[0][place, side, HD + 8 :, :] = jnp.broadcast_to(top, total.shape)


def absorb(asking, blocks, heads, state, last):
    rows = asking[0].shape[1]
    keys = blocks[0].shape[1] * len(blocks)
    count = len(heads)
    first = state is None
    if last:
        shape = jax.ShapeDtypeStruct((rows, count * HD), jnp.bfloat16)
        out_shape, out_specs = (shape, shape), (VMEM, VMEM)
    else:
        out_shape = jax.ShapeDtypeStruct((count, 2, STATE, rows), jnp.float32)
        out_specs = VMEM
    operands = [*asking, *blocks] + ([] if first else [state])
    return pl.pallas_call(
        functools.partial(absorb_kernel, heads, len(blocks), first, last),
        out_shape=out_shape,
        in_specs=[VMEM] * len(operands),
        out_specs=out_specs,
        input_output_aliases={} if first or last else {len(operands) - 1: 0},
        cost_estimate=pl.CostEstimate(
            flops=8 * count * rows * keys * HD,
            bytes_accessed=count * rows * HD * 12,
            transcendentals=2 * count * rows * keys,
        ),
        compiler_params=limit(12),
        name="absorb",
    )(*operands)


def project_kernel(pieces, *refs):
    out = refs[-1]
    refs = refs[1:-1]
    left = jnp.concatenate([refs[2 * at][...] for at in range(pieces)], axis=1)
    right = jnp.concatenate([refs[2 * at + 1][...] for at in range(pieces)], axis=0)
    base, gate = refs[-2], refs[-1]
    branch = jnp.dot(left, right, preferred_element_type=jnp.float32)
    out[...] = (base[...].astype(jnp.float32) + gate[...] * branch).astype(out.dtype)


def finish_kernel(pieces, wide, *refs):
    lefts, rights = refs[:pieces], refs[pieces : 2 * pieces]
    base, gate, out, held, sems = refs[2 * pieces :]
    left = jnp.concatenate([ref[...] for ref in lefts], axis=1)
    copies = []
    for at in range(base.shape[1] // wide):
        lanes = slice(at * wide, (at + 1) * wide)
        right = jnp.concatenate([ref[:, lanes] for ref in rights], axis=0)
        branch = jnp.dot(left, right, preferred_element_type=jnp.float32)
        held[:, lanes] = (base[:, lanes] + gate[:, lanes] * branch).astype(held.dtype)
        copies.append(pltpu.make_async_copy(held.at[:, lanes], out.at[:, lanes], sems.at[at]))
        copies[-1].start()
    for copy in copies:
        copy.wait()


def finish(pieces, weights, base, gate, wide):
    operands = [*pieces, *weights, base, gate]
    return pl.pallas_call(
        functools.partial(finish_kernel, len(pieces), wide),
        out_shape=jax.ShapeDtypeStruct(base.shape, jnp.bfloat16),
        in_specs=[VMEM] * len(operands),
        out_specs=ANY,
        scratch_shapes=[
            pltpu.VMEM(base.shape, jnp.bfloat16),
            pltpu.SemaphoreType.DMA((base.shape[1] // wide,)),
        ],
        cost_estimate=pl.CostEstimate(
            flops=2 * len(pieces) * HD * base.size, bytes_accessed=base.size * 2, transcendentals=0
        ),
        compiler_params=limit(12),
        name="finish",
    )(*operands)


def project(where, sources, base, gate, cols, wide, dtype):
    rows = base.shape[0]
    steps = cols // wide
    operands, specs, depth = [], [], 0
    for piece, lane, weight, row, whole in sources:
        width = piece.shape[1] if lane is None else HD
        depth += width

        def left(j, s, lane=lane):
            return 0, (0 if lane is None else lane(s))

        def right(j, s, row=row, whole=whole):
            return row(s), (s[0] * steps + j if whole else j)

        operands += [piece, weight]
        specs += [pl.BlockSpec((rows, width), left), pl.BlockSpec((width, wide), right)]
    whole = base.shape[1] != cols
    operands += [base, gate]
    specs += [
        pl.BlockSpec((rows, wide), lambda j, s: (0, s[0] * steps + j if whole else j)),
        pl.BlockSpec((1, wide), lambda j, s: (0, s[0] * steps + j)),
    ]
    return pl.pallas_call(
        functools.partial(project_kernel, len(sources)),
        out_shape=jax.ShapeDtypeStruct((rows, cols), dtype),
        grid_spec=pltpu.PrefetchScalarGridSpec(
            num_scalar_prefetch=1,
            grid=(steps,),
            in_specs=specs,
            out_specs=pl.BlockSpec((rows, wide), lambda j, s: (0, j)),
        ),
        cost_estimate=pl.CostEstimate(
            flops=2 * rows * depth * cols, bytes_accessed=rows * cols * 4, transcendentals=0
        ),
        compiler_params=limit(12),
        name="project",
    )(where, *operands)


def role_of(member):
    return (member // 2 + 1) // 2 % 2


def per_device(stream_in, queries, keys, values, out_weight, gate_scale):
    sections = lax.axis_size("segment")
    seq_count = lax.axis_size("seq")
    shares = lax.axis_size("head")
    local = queries.shape[2] // HD // 2
    cycle_len = min(32, seq_count)
    stride = seq_count // cycle_len
    planes = cycle_len // 2
    rounds = planes // 2

    partner = {m: m ^ 2 for m in range(cycle_len)}
    beside = {m: m ^ 1 for m in range(cycle_len)}
    beyond = {}
    for role in range(2):
        for column in range(2):
            line = [p * 2 + column for p in range(planes) if role_of(p * 2) == role]
            for at, m in enumerate(line):
                beyond[m] = line[(at + 1) % len(line)]

    def hop(block, towards, shift=0, by=0):
        pairs = []
        for section in range(sections):
            for member in range(cycle_len):
                for video in range(stride):
                    for share in range(shares):
                        origin = section * seq_count + member * stride + video
                        target = (
                            (section + shift) % sections * seq_count
                            + towards[member] * stride
                            + video
                        )
                        pairs.append(
                            (origin * shares + share, target * shares + (share + by) % shares)
                        )
        return lax.ppermute(block, ("segment", "seq", "head"), pairs)

    still = {m: m for m in range(cycle_len)}
    share = lax.axis_index("head").astype(jnp.int32)
    role = role_of(lax.axis_index("seq").astype(jnp.int32) // stride)
    role_ref = role.reshape(1)
    column = lax.axis_index("seq").astype(jnp.int32) // stride % 2
    where = jnp.stack([share, role, column])
    groups = [(0, 1), (2,)]
    everyone = range(len(groups))

    col_count = out_weight.shape[2] // shares
    lent = {}
    for by in range(1, shares):
        start = lax.rem(share + by, shares) * col_count
        lent[by] = []
        for head, count in ((role * local + 2, 1), (role * local, 2), ((1 - role) * local, 2)):
            part = lax.dynamic_slice(out_weight[0], (head * HD, start), (count * HD, col_count))
            lent[by].append(hop(part, still, 1, by))

    packed = pack(role_ref, keys[0], values[0], groups)
    mine, give = packed[: len(groups)], packed[len(groups) :]
    my_query, give_query = turned(role_ref, queries[0])
    got = [None] * len(groups)
    far = [[None] * 2 for _ in groups]
    near = [[None] * 2 for _ in groups]
    own = [None] * len(groups)
    everyone = range(len(groups))
    for g in everyone:
        got[g] = hop(give[g], partner, 1)
        far[g][0] = hop(mine[g], beyond, 1)
        near[g][0] = hop(mine[g], beside, 1)
        own[g] = hop(mine[g], still, 1)
    asking = [hop(my_query, still, 1), hop(give_query, partner, 1)]
    weight = hop(out_weight[0], still, 1)
    stream = hop(stream_in[0], still, 1)
    gate = hop(gate_scale, still, 1)
    for by in range(1, shares):
        lent[by].append(hop(lent[by][0], partner))

    def fold(g, blocks, held, last=False):
        return absorb(asking, blocks, groups[g], held, last)

    attended = []
    for g in everyone:
        far[g][1] = hop(got[g], beyond)
        near[g][1] = hop(got[g], beside)
        state = fold(g, [own[g], got[g]], None)
        state = fold(g, near[g], state)
        arrived = far[g]
        for turn in range(1, rounds):
            onward = [hop(arrived[i], beside) for i in range(2)]
            following = None
            if turn < rounds - 1:
                following = [hop(arrived[i], beyond) for i in range(2)]
            state = fold(g, arrived, state)
            if turn < rounds - 1:
                state = fold(g, onward, state)
            elif g < len(groups) - 1:
                attended.append(fold(g, onward, state, True))
            else:
                state = fold(g, onward[:1], state)
                attended.append(fold(g, onward[1:], state, True))
            arrived = following

    home = []
    for g in everyone:
        ours, theirs = attended[g]
        back = hop(theirs, partner)
        over = {by: hop(ours, still, 0, by) for by in range(1, shares)}
        cross = {by: hop(theirs, partner, 0, by) for by in range(1, shares)}
        home.append((ours, back, over, cross))

    def top(s):
        return 0

    first, second = home
    sources = []
    for head in range(2):
        pick = lambda s, head=head: head
        sources.append((first[0], pick, weight, lambda s, h=head: s[1] * local + h, True))
        sources.append((first[1], pick, weight, lambda s, h=head: (1 - s[1]) * local + h, True))
    sources.append((second[0], None, weight, lambda s: s[1] * local + 2, True))
    own_start = share * col_count
    last_pieces = [second[1]]
    last_weights = [
        lax.dynamic_slice(weight, (((1 - role) * local + 2) * HD, own_start), (HD, col_count))
    ]
    for by in range(1, shares):
        thirds, pairs, others, relayed = lent[by]
        sources.append((first[2][by], None, pairs, top, False))
        sources.append((first[3][by], None, others, top, False))
        last_pieces += [second[2][by], second[3][by]]
        last_weights += [thirds, relayed]
    base = project(where, sources, stream, gate, col_count, 512, jnp.float32)
    own_gate = lax.dynamic_slice(gate, (0, own_start), (1, col_count))
    return finish(last_pieces, last_weights, base, own_gate, 384)[None]


def solution(mesh):
    return jax.shard_map(
        per_device,
        mesh=mesh,
        in_specs=(
            P("segment", "seq", None),
            P("segment", "seq", "head"),
            P("segment", "seq", "head"),
            P("segment", "seq", "head"),
            P("segment", "head", None),
            P("segment", None),
        ),
        out_specs=P("segment", "seq", "head"),
        check_vma=False,
    )
```

```python
import functools
import math

import jax
import jax.numpy as jnp
from jax import lax
from jax.experimental import pallas as pl
from jax.experimental.pallas import tpu as pltpu
from jax.sharding import PartitionSpec as P


HD = 128
STATE = HD + 16
LOG2E = 1.4426950408889634
VMEM = pl.BlockSpec(memory_space=pltpu.VMEM)


def limit(mib):
    return pltpu.CompilerParams(vmem_limit_bytes=mib << 20)


def pack_kernel(groups, role_ref, k_any, v_any, q_any, *rest):
    outs, (k_ref, v_ref, q_ref, sems) = rest[:-4], rest[-4:]
    loads = [
        pltpu.make_async_copy(source, target, sems.at[at])
        for at, (source, target) in enumerate(((k_any, k_ref), (v_any, v_ref), (q_any, q_ref)))
    ]
    for load in loads:
        load.start()
    rows, width = k_ref.shape
    half = width // 2
    loads[0].wait()
    loads[1].wait()
    for side in range(2):
        role = role_ref[0] if side == 0 else 1 - role_ref[0]
        for heads, out in zip(groups, outs[side * len(groups) :]):
            for place, head in enumerate(heads):
                lanes = pl.ds(pl.multiple_of(role * half + head * HD, HD), HD)
                base = place * 2 * HD
                for piece in range(rows // HD):
                    out[base : base + HD, piece * HD : (piece + 1) * HD] = k_ref[
                        piece * HD : (piece + 1) * HD, lanes
                    ]
                out[base + HD : base + 2 * HD, :] = v_ref[:, lanes].T
    loads[2].wait()
    for side in range(2):
        role = role_ref[0] if side == 0 else 1 - role_ref[0]
        for head in range(half // HD):
            lanes = pl.ds(pl.multiple_of(role * half + head * HD, HD), HD)
            outs[side - 2][head * HD : (head + 1) * HD, :] = q_ref[:, lanes].T


SMEM = pl.BlockSpec(memory_space=pltpu.SMEM)
ANY = pl.BlockSpec(memory_space=pl.ANY)


def in_hbm(x):
    return pltpu.with_memory_space_constraint(x, pltpu.HBM)


def pack(role, keys, values, queries, groups):
    rows, width = keys.shape
    shapes = [
        jax.ShapeDtypeStruct((len(heads) * 2 * HD, rows), jnp.bfloat16) for heads in groups
    ]
    asked = jax.ShapeDtypeStruct((width // 2, rows), jnp.bfloat16)
    return pl.pallas_call(
        functools.partial(pack_kernel, groups),
        out_shape=tuple(shapes + shapes + [asked, asked]),
        in_specs=[SMEM, ANY, ANY, ANY],
        out_specs=(VMEM,) * (2 * len(groups) + 2),
        scratch_shapes=[pltpu.VMEM((rows, width), jnp.bfloat16)] * 3
        + [pltpu.SemaphoreType.DMA((3,))],
        compiler_params=limit(8),
        name="pack",
    )(role, in_hbm(keys), in_hbm(values), in_hbm(queries))


def carve_kernel(local, cols, spot_ref, w_any, third_ref, firsts_ref, sems):
    role, share = spot_ref[0], spot_ref[1]
    lanes = pl.ds(pl.multiple_of(share * cols, HD), cols)
    pair = 2 * HD

    def rows(head, count):
        return w_any.at[pl.ds(pl.multiple_of(head * HD, HD), count), lanes]

    copies = [
        pltpu.make_async_copy(rows(role * local + 2, HD), third_ref, sems.at[0]),
        pltpu.make_async_copy(rows(role * local, pair), firsts_ref.at[:pair, :], sems.at[1]),
        pltpu.make_async_copy(rows((1 - role) * local, pair), firsts_ref.at[pair:, :], sems.at[2]),
    ]
    for copy in copies:
        copy.start()
    for copy in copies:
        copy.wait()


def carve(spot, weight, local, cols):
    return pl.pallas_call(
        functools.partial(carve_kernel, local, cols),
        out_shape=(
            jax.ShapeDtypeStruct((HD, cols), weight.dtype),
            jax.ShapeDtypeStruct((4 * HD, cols), weight.dtype),
        ),
        in_specs=[SMEM, ANY],
        out_specs=(VMEM, VMEM),
        scratch_shapes=[pltpu.SemaphoreType.DMA((3,))],
        compiler_params=limit(4),
        name="carve",
    )(spot, in_hbm(weight))


def absorb_kernel(heads, count, first, last, *refs):
    q_refs, kv_refs, rest = refs[:2], refs[2 : 2 + count], refs[2 + count :]
    state = None if first else rest[0]
    outs = rest if first else rest[1:]
    keys = kv_refs[0].shape[1]
    factor = LOG2E / math.sqrt(HD)
    for place, head in enumerate(heads):
        base = place * 2 * HD
        key = jnp.concatenate(
            [
                kv[base : base + HD, piece * HD : (piece + 1) * HD]
                for kv in kv_refs
                for piece in range(keys // HD)
            ],
            axis=0,
        )
        value = jnp.concatenate([kv[base + HD : base + 2 * HD, :] for kv in kv_refs], axis=1)
        tall = jnp.concatenate([value, jnp.ones((16, value.shape[1]), jnp.bfloat16)], axis=0)
        for side, q_ref in enumerate(q_refs):
            query = q_ref[head * HD : (head + 1) * HD, :]
            scores = jnp.dot(key, query, preferred_element_type=jnp.float32)
            top = jnp.max(scores, axis=0, keepdims=True)
            if not first:
                top_old = state[place, side, HD + 8 : HD + 9, :]
                top = jnp.maximum(top_old, top)
            raised = jnp.exp2((scores - top) * factor).astype(jnp.bfloat16)
            both = jnp.dot(tall, raised, preferred_element_type=jnp.float32)
            mixed, total = both[:HD], both[HD : HD + 8]
            if not first:
                shrink = jnp.exp2((top_old - top) * factor)
                mixed = state[place, side, :HD, :] * shrink + mixed
                total = state[place, side, HD : HD + 8, :] * shrink + total
            if last:
                done = mixed / total[:1]
                outs[side][:, place * HD : (place + 1) * HD] = done.T.astype(jnp.bfloat16)
            else:
                outs[0][place, side, :HD, :] = mixed
                outs[0][place, side, HD : HD + 8, :] = total
                outs[0][place, side, HD + 8 :, :] = jnp.broadcast_to(top, total.shape)


def absorb(asking, blocks, heads, state, last):
    rows = asking[0].shape[1]
    keys = blocks[0].shape[1] * len(blocks)
    count = len(heads)
    first = state is None
    if last:
        shape = jax.ShapeDtypeStruct((rows, count * HD), jnp.bfloat16)
        out_shape, out_specs = (shape, shape), (VMEM, VMEM)
    else:
        out_shape = jax.ShapeDtypeStruct((count, 2, STATE, rows), jnp.float32)
        out_specs = VMEM
    operands = [*asking, *blocks] + ([] if first else [state])
    return pl.pallas_call(
        functools.partial(absorb_kernel, heads, len(blocks), first, last),
        out_shape=out_shape,
        in_specs=[VMEM] * len(operands),
        out_specs=out_specs,
        input_output_aliases={} if first or last else {len(operands) - 1: 0},
        cost_estimate=pl.CostEstimate(
            flops=8 * count * rows * keys * HD,
            bytes_accessed=count * rows * HD * 12,
            transcendentals=2 * count * rows * keys,
        ),
        compiler_params=limit(12),
        name="absorb",
    )(*operands)


def project_kernel(pieces, *refs):
    out, kept, kept_gate = refs[-3:]
    refs = refs[1:-3]
    left = jnp.concatenate([refs[2 * at][...] for at in range(pieces)], axis=1)
    right = jnp.concatenate([refs[2 * at + 1][...] for at in range(pieces)], axis=0)
    keep, stream, gate = refs[-3:]
    branch = jnp.dot(left, right, preferred_element_type=jnp.float32)
    out[...] = stream[...].astype(jnp.float32) + gate[...] * branch
    kept[...] = keep[...]
    kept_gate[...] = gate[...]


def finish_kernel(pieces, wide, *refs):
    lefts, rights = refs[:pieces], refs[pieces : 2 * pieces]
    base, gate, out, held, sems = refs[2 * pieces :]
    left = jnp.concatenate([ref[...] for ref in lefts], axis=1)
    copies = []
    for at in range(base.shape[1] // wide):
        lanes = slice(at * wide, (at + 1) * wide)
        right = jnp.concatenate([ref[:, lanes] for ref in rights], axis=0)
        branch = jnp.dot(left, right, preferred_element_type=jnp.float32)
        held[:, lanes] = (base[:, lanes] + gate[:, lanes] * branch).astype(held.dtype)
        copies.append(pltpu.make_async_copy(held.at[:, lanes], out.at[:, lanes], sems.at[at]))
        copies[-1].start()
    for copy in copies:
        copy.wait()


def finish(pieces, weights, base, gate, wide):
    operands = [*pieces, *weights, base, gate]
    return pl.pallas_call(
        functools.partial(finish_kernel, len(pieces), wide),
        out_shape=jax.ShapeDtypeStruct(base.shape, jnp.bfloat16),
        in_specs=[VMEM] * len(operands),
        out_specs=ANY,
        scratch_shapes=[
            pltpu.VMEM(base.shape, jnp.bfloat16),
            pltpu.SemaphoreType.DMA((base.shape[1] // wide,)),
        ],
        cost_estimate=pl.CostEstimate(
            flops=2 * len(pieces) * HD * base.size, bytes_accessed=base.size * 2, transcendentals=0
        ),
        compiler_params=limit(12),
        name="finish",
    )(*operands)


def project(where, sources, keep, weight, stream, gate, cols, wide):
    rows = stream.shape[0]
    steps = cols // wide
    operands, specs, depth = [], [], 0

    def ours(j, s):
        return s[0] * steps + j

    for piece, lane, weights, row, whole in sources:
        width = piece.shape[1] if lane is None else HD
        depth += width

        def left(j, s, lane=lane):
            return 0, (0 if lane is None else lane)

        def right(j, s, row=row, whole=whole):
            return row(s), (ours(j, s) if whole else j)

        operands += [piece, weights]
        specs += [pl.BlockSpec((rows, width), left), pl.BlockSpec((width, wide), right)]
    operands += [weight, stream, gate]
    specs += [
        pl.BlockSpec((HD, wide), lambda j, s: (keep(s), ours(j, s))),
        pl.BlockSpec((rows, wide), lambda j, s: (0, ours(j, s))),
        pl.BlockSpec((1, wide), lambda j, s: (0, ours(j, s))),
    ]
    return pl.pallas_call(
        functools.partial(project_kernel, len(sources)),
        out_shape=(
            jax.ShapeDtypeStruct((rows, cols), jnp.float32),
            jax.ShapeDtypeStruct((HD, cols), weight.dtype),
            jax.ShapeDtypeStruct((1, cols), gate.dtype),
        ),
        grid_spec=pltpu.PrefetchScalarGridSpec(
            num_scalar_prefetch=1,
            grid=(steps,),
            in_specs=specs,
            out_specs=(
                pl.BlockSpec((rows, wide), lambda j, s: (0, j)),
                pl.BlockSpec((HD, wide), lambda j, s: (0, j)),
                pl.BlockSpec((1, wide), lambda j, s: (0, j)),
            ),
        ),
        cost_estimate=pl.CostEstimate(
            flops=2 * rows * depth * cols, bytes_accessed=rows * cols * 4, transcendentals=0
        ),
        compiler_params=limit(12),
        name="project",
    )(where, *operands)


def role_of(member):
    return (member // 2 + 1) // 2 % 2


def per_device(stream_in, queries, keys, values, out_weight, gate_scale):
    sections = lax.axis_size("segment")
    seq_count = lax.axis_size("seq")
    shares = lax.axis_size("head")
    local = queries.shape[2] // HD // 2
    cycle_len = min(32, seq_count)
    stride = seq_count // cycle_len
    planes = cycle_len // 2
    rounds = planes // 2

    partner = {m: m ^ 2 for m in range(cycle_len)}
    beside = {m: m ^ 1 for m in range(cycle_len)}
    beyond = {}
    for role in range(2):
        for column in range(2):
            line = [p * 2 + column for p in range(planes) if role_of(p * 2) == role]
            for at, m in enumerate(line):
                beyond[m] = line[(at + 1) % len(line)]

    def hop(block, towards, shift=0, by=0):
        pairs = []
        for section in range(sections):
            for member in range(cycle_len):
                for video in range(stride):
                    for share in range(shares):
                        origin = section * seq_count + member * stride + video
                        target = (
                            (section + shift) % sections * seq_count
                            + towards[member] * stride
                            + video
                        )
                        pairs.append(
                            (origin * shares + share, target * shares + (share + by) % shares)
                        )
        return lax.ppermute(block, ("segment", "seq", "head"), pairs)

    still = {m: m for m in range(cycle_len)}
    share = lax.axis_index("head").astype(jnp.int32)
    role = role_of(lax.axis_index("seq").astype(jnp.int32) // stride)
    role_ref = role.reshape(1)
    where = jnp.stack([share, role])
    groups = [(0, 1), (2,)]

    packed = pack(role_ref, keys[0], values[0], queries[0], groups)
    mine, give = packed[: len(groups)], packed[len(groups) : 2 * len(groups)]
    my_query, give_query = packed[-2:]
    got = [None] * len(groups)
    far = [[None] * 2 for _ in groups]
    near = [[None] * 2 for _ in groups]
    own = [None] * len(groups)
    everyone = range(len(groups))
    for g in everyone:
        got[g] = hop(give[g], partner, 1)
        far[g][0] = hop(mine[g], beyond, 1)
        near[g][0] = hop(mine[g], beside, 1)
        own[g] = hop(mine[g], still, 1)
    asking = [hop(my_query, still, 1), hop(give_query, partner, 1)]

    col_count = out_weight.shape[2] // shares
    lent = {}
    for by in range(1, shares):
        spot = jnp.stack([role, lax.rem(share + by, shares)])
        parts = carve(spot, out_weight[0], local, col_count)
        lent[by] = [hop(part, still, 1, by) for part in parts]
        lent[by].append(hop(lent[by][0], partner))
    weight = hop(out_weight[0], still, 1)
    stream = hop(stream_in[0], still, 1)
    gate = hop(gate_scale, still, 1)

    def fold(g, blocks, held, last=False):
        return absorb(asking, blocks, groups[g], held, last)

    attended = []
    for g in everyone:
        far[g][1] = hop(got[g], beyond)
        near[g][1] = hop(got[g], beside)
        state = fold(g, [own[g], got[g], *near[g]], None)
        arrived = far[g]
        for turn in range(1, rounds):
            onward = [hop(arrived[i], beside) for i in range(2)]
            state = fold(g, [arrived[0], onward[0], arrived[1]], state)
            if turn < rounds - 1:
                state = fold(g, onward[1:], state)
                arrived = [hop(arrived[i], beyond) for i in range(2)]
            else:
                attended.append(fold(g, onward[1:], state, True))

    home = []
    for g in everyone:
        ours, theirs = attended[g]
        back = hop(theirs, partner)
        over = {by: hop(ours, still, 0, by) for by in range(1, shares)}
        cross = {by: hop(theirs, partner, 0, by) for by in range(1, shares)}
        home.append((ours, back, over, cross))

    def top(s):
        return 0

    first, second = home
    sources = []
    for head in range(2):
        sources.append((first[0], head, weight, lambda s, h=head: s[1] * local + h, True))
        sources.append((first[1], head, weight, lambda s, h=head: (1 - s[1]) * local + h, True))
    sources.append((second[0], None, weight, lambda s: s[1] * local + 2, True))
    for by in range(1, shares):
        firsts = lent[by][1]
        sources.append((first[2][by], None, firsts, top, False))
        sources.append((first[3][by], None, firsts, lambda s: 1, False))
    base, own_third, own_gate = project(
        where, sources, lambda s: (1 - s[1]) * local + 2, weight, stream, gate, col_count, 512
    )
    last_pieces, last_weights = [second[1]], [own_third]
    for by in range(1, shares):
        last_pieces += [second[2][by], second[3][by]]
        last_weights += [lent[by][0], lent[by][2]]
    return finish(last_pieces, last_weights, base, own_gate, 384)[None]


def solution(mesh):
    return jax.shard_map(
        per_device,
        mesh=mesh,
        in_specs=(
            P("segment", "seq", None),
            P("segment", "seq", "head"),
            P("segment", "seq", "head"),
            P("segment", "seq", "head"),
            P("segment", "head", None),
            P("segment", None),
        ),
        out_specs=P("segment", "seq", "head"),
        check_vma=False,
    )
```

```python
import functools
import math

import jax
import jax.numpy as jnp
from jax import lax
from jax.experimental import pallas as pl
from jax.experimental.pallas import tpu as pltpu
from jax.sharding import PartitionSpec as P


HD = 128
STATE = HD + 16
LOG2E = 1.4426950408889634
VMEM = pl.BlockSpec(memory_space=pltpu.VMEM)


def limit(mib):
    return pltpu.CompilerParams(vmem_limit_bytes=mib << 20)


def pack_kernel(groups, local, cols, spot_ref, k_any, v_any, q_any, w_any, *rest):
    outs, (k_ref, v_ref, q_ref, sems) = rest[:-4], rest[-4:]
    mine_role = spot_ref[0]
    third = w_any.at[
        pl.ds(pl.multiple_of((mine_role * local + 2) * HD, HD), HD),
        pl.ds(pl.multiple_of(spot_ref[1] * cols, HD), cols),
    ]
    loads = [
        pltpu.make_async_copy(source, target, sems.at[at])
        for at, (source, target) in enumerate(
            ((k_any, k_ref), (v_any, v_ref), (q_any, q_ref), (third, outs[-1]))
        )
    ]
    for load in loads:
        load.start()
    rows, width = k_ref.shape
    half = width // 2
    loads[0].wait()
    loads[1].wait()
    for side in range(2):
        role = mine_role if side == 0 else 1 - mine_role
        for heads, out in zip(groups, outs[side * len(groups) :]):
            for place, head in enumerate(heads):
                lanes = pl.ds(pl.multiple_of(role * half + head * HD, HD), HD)
                base = place * 2 * HD
                for piece in range(rows // HD):
                    out[base : base + HD, piece * HD : (piece + 1) * HD] = k_ref[
                        piece * HD : (piece + 1) * HD, lanes
                    ]
                out[base + HD : base + 2 * HD, :] = v_ref[:, lanes].T
    loads[2].wait()
    for side in range(2):
        role = mine_role if side == 0 else 1 - mine_role
        for head in range(half // HD):
            lanes = pl.ds(pl.multiple_of(role * half + head * HD, HD), HD)
            outs[side - 3][head * HD : (head + 1) * HD, :] = q_ref[:, lanes].T
    loads[3].wait()


SMEM = pl.BlockSpec(memory_space=pltpu.SMEM)
ANY = pl.BlockSpec(memory_space=pl.ANY)


def in_hbm(x):
    return pltpu.with_memory_space_constraint(x, pltpu.HBM)


def pack(spot, keys, values, queries, weight, groups, cols):
    rows, width = keys.shape
    shapes = [
        jax.ShapeDtypeStruct((len(heads) * 2 * HD, rows), jnp.bfloat16) for heads in groups
    ]
    asked = jax.ShapeDtypeStruct((width // 2, rows), jnp.bfloat16)
    third = jax.ShapeDtypeStruct((HD, cols), jnp.bfloat16)
    return pl.pallas_call(
        functools.partial(pack_kernel, groups, width // 2 // HD, cols),
        out_shape=tuple(shapes + shapes + [asked, asked, third]),
        in_specs=[SMEM, ANY, ANY, ANY, ANY],
        out_specs=(VMEM,) * (2 * len(groups) + 3),
        scratch_shapes=[pltpu.VMEM((rows, width), jnp.bfloat16)] * 3
        + [pltpu.SemaphoreType.DMA((4,))],
        compiler_params=limit(8),
        name="pack",
    )(spot, in_hbm(keys), in_hbm(values), in_hbm(queries), in_hbm(weight))


def carve_kernel(local, cols, heads, spot_ref, w_any, *rest):
    out, sems = rest
    lanes = pl.ds(pl.multiple_of(spot_ref[1] * cols, HD), cols)
    unit = HD // 2
    copies = []
    for at, (ours, head) in enumerate(heads):
        role = spot_ref[0] if ours else 1 - spot_ref[0]
        for part in range(2):
            row = pl.multiple_of((role * local + head) * HD + part * unit, unit)
            to = at * HD + part * unit
            copies.append(
                pltpu.make_async_copy(
                    w_any.at[pl.ds(row, unit), lanes],
                    out.at[to : to + unit, :],
                    sems.at[2 * at + part],
                )
            )
    for copy in copies:
        copy.start()
    for copy in copies:
        copy.wait()


def carve(spot, weight, local, cols, heads):
    return pl.pallas_call(
        functools.partial(carve_kernel, local, cols, heads),
        out_shape=jax.ShapeDtypeStruct((len(heads) * HD, cols), weight.dtype),
        in_specs=[SMEM, ANY],
        out_specs=VMEM,
        scratch_shapes=[pltpu.SemaphoreType.DMA((2 * len(heads),))],
        compiler_params=limit(4),
        name="carve",
    )(spot, in_hbm(weight))


def absorb_kernel(heads, count, first, last, *refs):
    q_refs, kv_refs, rest = refs[:2], refs[2 : 2 + count], refs[2 + count :]
    state = None if first else rest[0]
    outs = rest if first else rest[1:]
    keys = kv_refs[0].shape[1]
    factor = LOG2E / math.sqrt(HD)
    for place, head in enumerate(heads):
        base = place * 2 * HD
        key = jnp.concatenate(
            [
                kv[base : base + HD, piece * HD : (piece + 1) * HD]
                for kv in kv_refs
                for piece in range(keys // HD)
            ],
            axis=0,
        )
        value = jnp.concatenate([kv[base + HD : base + 2 * HD, :] for kv in kv_refs], axis=1)
        tall = jnp.concatenate([value, jnp.ones((16, value.shape[1]), jnp.bfloat16)], axis=0)
        for side, q_ref in enumerate(q_refs):
            query = q_ref[head * HD : (head + 1) * HD, :]
            scores = jnp.dot(key, query, preferred_element_type=jnp.float32)
            top = jnp.max(scores, axis=0, keepdims=True)
            if not first:
                top_old = state[place, side, HD + 8 : HD + 9, :]
                top = jnp.maximum(top_old, top)
            raised = jnp.exp2((scores - top) * factor).astype(jnp.bfloat16)
            both = jnp.dot(tall, raised, preferred_element_type=jnp.float32)
            mixed, total = both[:HD], both[HD : HD + 8]
            if not first:
                shrink = jnp.exp2((top_old - top) * factor)
                mixed = state[place, side, :HD, :] * shrink + mixed
                total = state[place, side, HD : HD + 8, :] * shrink + total
            if last:
                done = mixed / total[:1]
                outs[side][:, place * HD : (place + 1) * HD] = done.T.astype(jnp.bfloat16)
            else:
                outs[0][place, side, :HD, :] = mixed
                outs[0][place, side, HD : HD + 8, :] = total
                outs[0][place, side, HD + 8 :, :] = jnp.broadcast_to(top, total.shape)


def absorb(asking, blocks, heads, state, last):
    rows = asking[0].shape[1]
    keys = blocks[0].shape[1] * len(blocks)
    count = len(heads)
    first = state is None
    if last:
        shape = jax.ShapeDtypeStruct((rows, count * HD), jnp.bfloat16)
        out_shape, out_specs = (shape, shape), (VMEM, VMEM)
    else:
        out_shape = jax.ShapeDtypeStruct((count, 2, STATE, rows), jnp.float32)
        out_specs = VMEM
    operands = [*asking, *blocks] + ([] if first else [state])
    return pl.pallas_call(
        functools.partial(absorb_kernel, heads, len(blocks), first, last),
        out_shape=out_shape,
        in_specs=[VMEM] * len(operands),
        out_specs=out_specs,
        input_output_aliases={} if first or last else {len(operands) - 1: 0},
        cost_estimate=pl.CostEstimate(
            flops=8 * count * rows * keys * HD,
            bytes_accessed=count * rows * HD * 12,
            transcendentals=2 * count * rows * keys,
        ),
        compiler_params=limit(12),
        name="absorb",
    )(*operands)


def project_kernel(pieces, *refs):
    out, kept, kept_gate = refs[-3:]
    refs = refs[1:-3]
    left = jnp.concatenate([refs[2 * at][...] for at in range(pieces)], axis=1)
    right = jnp.concatenate([refs[2 * at + 1][...] for at in range(pieces)], axis=0)
    keep, stream, gate = refs[-3:]
    branch = jnp.dot(left, right, preferred_element_type=jnp.float32)
    out[...] = stream[...].astype(jnp.float32) + gate[...] * branch
    kept[...] = keep[...]
    kept_gate[...] = gate[...]


def middle_kernel(pieces, wide, *refs):
    lefts, rights = refs[:pieces], refs[pieces : pieces + 1]
    base, gate, out = refs[pieces + 1 :]
    left = jnp.concatenate([ref[...] for ref in lefts], axis=1)
    for at in range(base.shape[1] // wide):
        lanes = slice(at * wide, (at + 1) * wide)
        right = jnp.concatenate([ref[:, lanes] for ref in rights], axis=0)
        branch = jnp.dot(left, right, preferred_element_type=jnp.float32)
        out[:, lanes] = base[:, lanes] + gate[:, lanes] * branch


def middle(pieces, weights, base, gate, wide):
    operands = [*pieces, *weights, base, gate]
    return pl.pallas_call(
        functools.partial(middle_kernel, len(pieces), wide),
        out_shape=jax.ShapeDtypeStruct(base.shape, jnp.float32),
        in_specs=[VMEM] * len(operands),
        out_specs=VMEM,
        input_output_aliases={len(operands) - 2: 0},
        cost_estimate=pl.CostEstimate(
            flops=4 * len(pieces) * HD * base.size, bytes_accessed=base.size, transcendentals=0
        ),
        compiler_params=limit(12),
        name="middle",
    )(*operands)


def finish_kernel(pieces, wide, *refs):
    lefts, rights = refs[:pieces], refs[pieces : 2 * pieces]
    base, gate, out, held, sems = refs[2 * pieces :]
    left = jnp.concatenate([ref[...] for ref in lefts], axis=1)
    copies = []
    for at in range(base.shape[1] // wide):
        lanes = slice(at * wide, (at + 1) * wide)
        right = jnp.concatenate([ref[:, lanes] for ref in rights], axis=0)
        branch = jnp.dot(left, right, preferred_element_type=jnp.float32)
        held[:, lanes] = (base[:, lanes] + gate[:, lanes] * branch).astype(held.dtype)
        copies.append(pltpu.make_async_copy(held.at[:, lanes], out.at[:, lanes], sems.at[at]))
        copies[-1].start()
    for copy in copies:
        copy.wait()


def finish(pieces, weights, base, gate, wide):
    operands = [*pieces, *weights, base, gate]
    return pl.pallas_call(
        functools.partial(finish_kernel, len(pieces), wide),
        out_shape=jax.ShapeDtypeStruct(base.shape, jnp.bfloat16),
        in_specs=[VMEM] * len(operands),
        out_specs=ANY,
        scratch_shapes=[
            pltpu.VMEM(base.shape, jnp.bfloat16),
            pltpu.SemaphoreType.DMA((base.shape[1] // wide,)),
        ],
        cost_estimate=pl.CostEstimate(
            flops=2 * len(pieces) * HD * base.size, bytes_accessed=base.size * 2, transcendentals=0
        ),
        compiler_params=limit(12),
        name="finish",
    )(*operands)


def project(where, sources, keep, weight, stream, gate, cols, wide):
    rows = stream.shape[0]
    steps = cols // wide
    operands, specs, depth = [], [], 0

    def ours(j, s):
        return s[0] * steps + j

    for piece, lane, weights, row, whole in sources:
        width = piece.shape[1] if lane is None else HD
        depth += width

        def left(j, s, lane=lane):
            return 0, (0 if lane is None else lane)

        def right(j, s, row=row, whole=whole):
            return row(s), (ours(j, s) if whole else j)

        operands += [piece, weights]
        specs += [pl.BlockSpec((rows, width), left), pl.BlockSpec((width, wide), right)]
    operands += [weight, stream, gate]
    specs += [
        pl.BlockSpec((HD, wide), lambda j, s: (keep(s), ours(j, s))),
        pl.BlockSpec((rows, wide), lambda j, s: (0, ours(j, s))),
        pl.BlockSpec((1, wide), lambda j, s: (0, ours(j, s))),
    ]
    return pl.pallas_call(
        functools.partial(project_kernel, len(sources)),
        out_shape=(
            jax.ShapeDtypeStruct((rows, cols), jnp.float32),
            jax.ShapeDtypeStruct((HD, cols), weight.dtype),
            jax.ShapeDtypeStruct((1, cols), gate.dtype),
        ),
        grid_spec=pltpu.PrefetchScalarGridSpec(
            num_scalar_prefetch=1,
            grid=(steps,),
            in_specs=specs,
            out_specs=(
                pl.BlockSpec((rows, wide), lambda j, s: (0, j)),
                pl.BlockSpec((HD, wide), lambda j, s: (0, j)),
                pl.BlockSpec((1, wide), lambda j, s: (0, j)),
            ),
        ),
        cost_estimate=pl.CostEstimate(
            flops=2 * rows * depth * cols, bytes_accessed=rows * cols * 4, transcendentals=0
        ),
        compiler_params=limit(12),
        name="project",
    )(where, *operands)


def role_of(member):
    return member // 2 % 2


def per_device(stream_in, queries, keys, values, out_weight, gate_scale):
    sections = lax.axis_size("segment")
    seq_count = lax.axis_size("seq")
    shares = lax.axis_size("head")
    local = queries.shape[2] // HD // 2
    cycle_len = min(32, seq_count)
    stride = seq_count // cycle_len
    planes = cycle_len // 2
    rounds = planes // 2

    partner = {m: m ^ 2 for m in range(cycle_len)}
    beside = {m: m ^ 1 for m in range(cycle_len)}
    beyond = {}
    for role in range(2):
        for column in range(2):
            line = [p * 2 + column for p in range(planes) if role_of(p * 2) == role]
            for at, m in enumerate(line):
                beyond[m] = line[(at + 1) % len(line)]

    def hop(block, towards, shift=0, by=0):
        pairs = []
        for section in range(sections):
            for member in range(cycle_len):
                for video in range(stride):
                    for share in range(shares):
                        origin = section * seq_count + member * stride + video
                        target = (
                            (section + shift) % sections * seq_count
                            + towards[member] * stride
                            + video
                        )
                        pairs.append(
                            (origin * shares + share, target * shares + (share + by) % shares)
                        )
        return lax.ppermute(block, ("segment", "seq", "head"), pairs)

    still = {m: m for m in range(cycle_len)}
    share = lax.axis_index("head").astype(jnp.int32)
    role = role_of(lax.axis_index("seq").astype(jnp.int32) // stride)
    where = jnp.stack([share, role])
    groups = [(0, 1), (2,)]

    col_count = out_weight.shape[2] // shares
    spots = {by: jnp.stack([role, lax.rem(share + by, shares)]) for by in range(1, shares)}
    packed = pack(
        spots[1], keys[0], values[0], queries[0], out_weight[0], groups, col_count
    )
    mine, give = packed[: len(groups)], packed[len(groups) : 2 * len(groups)]
    my_query, give_query, own_thirds = packed[-3:]
    got = [None] * len(groups)
    far = [[None] * 2 for _ in groups]
    near = [[None] * 2 for _ in groups]
    own = [None] * len(groups)
    everyone = range(len(groups))
    for g in everyone:
        got[g] = hop(give[g], partner, 1)
        far[g][0] = hop(mine[g], beyond, 1)
        near[g][0] = hop(mine[g], beside, 1)
        own[g] = hop(mine[g], still, 1)
    asking = [hop(my_query, still, 1), hop(give_query, partner, 1)]

    lent = {}
    pairs = ((True, 0), (True, 1), (False, 0), (False, 1))
    for by in range(1, shares):
        part = own_thirds
        if by > 1:
            part = carve(spots[by], out_weight[0], local, col_count, ((True, 2),))
        lent[by] = [hop(part, still, 1, by)]
        part = carve(spots[by], out_weight[0], local, col_count, pairs)
        lent[by].append(hop(part, still, 1, by))
        lent[by].append(hop(lent[by][0], partner))
    weight = hop(out_weight[0], still, 1)
    stream = hop(stream_in[0], still, 1)
    gate = hop(gate_scale, still, 1)

    def fold(g, blocks, held, last=False):
        return absorb(asking, blocks, groups[g], held, last)

    attended = []
    for g in everyone:
        far[g][1] = hop(got[g], beyond)
        near[g][1] = hop(got[g], beside)
        state = fold(g, [own[g], got[g], *near[g]], None)
        arrived = far[g]
        for turn in range(1, rounds):
            onward = [hop(arrived[i], beside) for i in range(2)]
            state = fold(g, [arrived[0], onward[0], arrived[1]], state)
            if turn < rounds - 1:
                state = fold(g, onward[1:], state)
                arrived = [hop(arrived[i], beyond) for i in range(2)]
            else:
                attended.append(fold(g, onward[1:], state, True))

    home = []
    for g in everyone:
        ours, theirs = attended[g]
        back = hop(theirs, partner)
        over = {by: hop(ours, still, 0, by) for by in range(1, shares)}
        cross = {by: hop(theirs, partner, 0, by) for by in range(1, shares)}
        home.append((ours, back, over, cross))

    first, second = home
    sources = []
    for head in range(2):
        sources.append((first[0], head, weight, lambda s, h=head: s[1] * local + h, True))
        sources.append((first[1], head, weight, lambda s, h=head: (1 - s[1]) * local + h, True))
    sources.append((second[0], None, weight, lambda s: s[1] * local + 2, True))
    base, own_third, own_gate = project(
        where, sources, lambda s: (1 - s[1]) * local + 2, weight, stream, gate, col_count, 512
    )
    last_pieces, last_weights = [second[1]], [own_third]
    for by in range(1, shares):
        base = middle([first[2][by], first[3][by]], [lent[by][1]], base, own_gate, 512)
        last_pieces += [second[2][by], second[3][by]]
        last_weights += [lent[by][0], lent[by][2]]
    return finish(last_pieces, last_weights, base, own_gate, 384)[None]


def solution(mesh):
    return jax.shard_map(
        per_device,
        mesh=mesh,
        in_specs=(
            P("segment", "seq", None),
            P("segment", "seq", "head"),
            P("segment", "seq", "head"),
            P("segment", "seq", "head"),
            P("segment", "head", None),
            P("segment", None),
        ),
        out_specs=P("segment", "seq", "head"),
        check_vma=False,
    )
```

```python
import functools
import math

import jax
import jax.numpy as jnp
from jax import lax
from jax.experimental import pallas as pl
from jax.experimental.pallas import tpu as pltpu
from jax.sharding import PartitionSpec as P


HD = 128
STATE = HD + 16
SHARED = 64
LOG2E = 1.4426950408889634
VMEM = pl.BlockSpec(memory_space=pltpu.VMEM)


def limit(mib):
    return pltpu.CompilerParams(vmem_limit_bytes=mib << 20)


def pack_kernel(groups, local, cols, spot_ref, k_any, v_any, q_any, w_any, *rest):
    outs, (k_ref, v_ref, q_ref, sems) = rest[:-4], rest[-4:]
    mine_role = spot_ref[0]
    lanes = pl.ds(pl.multiple_of(spot_ref[1] * cols, HD), cols)
    third = w_any.at[pl.ds(pl.multiple_of((mine_role * local + 2) * HD, HD), HD), lanes]
    start = w_any.at[pl.ds(pl.multiple_of(mine_role * local * HD, HD), SHARED), lanes]
    loads = [
        pltpu.make_async_copy(source, target, sems.at[at])
        for at, (source, target) in enumerate(
            (
                (k_any, k_ref),
                (v_any, v_ref),
                (q_any, q_ref),
                (third, outs[-1].at[:HD, :]),
                (start, outs[-1].at[HD:, :]),
            )
        )
    ]
    for load in loads:
        load.start()
    rows, width = k_ref.shape
    half = width // 2
    loads[0].wait()
    loads[1].wait()
    for side in range(2):
        role = mine_role if side == 0 else 1 - mine_role
        for heads, out in zip(groups, outs[side * len(groups) :]):
            for place, head in enumerate(heads):
                lanes = pl.ds(pl.multiple_of(role * half + head * HD, HD), HD)
                base = place * 2 * HD
                for piece in range(rows // HD):
                    out[base : base + HD, piece * HD : (piece + 1) * HD] = k_ref[
                        piece * HD : (piece + 1) * HD, lanes
                    ]
                out[base + HD : base + 2 * HD, :] = v_ref[:, lanes].T
    loads[2].wait()
    for side in range(2):
        role = mine_role if side == 0 else 1 - mine_role
        for head in range(half // HD):
            lanes = pl.ds(pl.multiple_of(role * half + head * HD, HD), HD)
            outs[side - 3][head * HD : (head + 1) * HD, :] = q_ref[:, lanes].T
    loads[3].wait()
    loads[4].wait()


SMEM = pl.BlockSpec(memory_space=pltpu.SMEM)
ANY = pl.BlockSpec(memory_space=pl.ANY)


def in_hbm(x):
    return pltpu.with_memory_space_constraint(x, pltpu.HBM)


def pack(spot, keys, values, queries, weight, groups, cols):
    rows, width = keys.shape
    shapes = [
        jax.ShapeDtypeStruct((len(heads) * 2 * HD, rows), jnp.bfloat16) for heads in groups
    ]
    asked = jax.ShapeDtypeStruct((width // 2, rows), jnp.bfloat16)
    third = jax.ShapeDtypeStruct((HD + SHARED, cols), jnp.bfloat16)
    return pl.pallas_call(
        functools.partial(pack_kernel, groups, width // 2 // HD, cols),
        out_shape=tuple(shapes + shapes + [asked, asked, third]),
        in_specs=[SMEM, ANY, ANY, ANY, ANY],
        out_specs=(VMEM,) * (2 * len(groups) + 3),
        scratch_shapes=[pltpu.VMEM((rows, width), jnp.bfloat16)] * 3
        + [pltpu.SemaphoreType.DMA((5,))],
        compiler_params=limit(8),
        name="pack",
    )(spot, in_hbm(keys), in_hbm(values), in_hbm(queries), in_hbm(weight))


def carve_kernel(local, cols, parts, spot_ref, w_any, *rest):
    out, sems = rest
    lanes = pl.ds(pl.multiple_of(spot_ref[1] * cols, HD), cols)
    unit = HD // 2
    copies, to = [], 0
    for ours, first, count in parts:
        role = spot_ref[0] if ours else 1 - spot_ref[0]
        for at in range(first, first + count, unit):
            row = pl.multiple_of(role * local * HD + at, unit)
            copies.append(
                pltpu.make_async_copy(
                    w_any.at[pl.ds(row, unit), lanes],
                    out.at[to : to + unit, :],
                    sems.at[len(copies)],
                )
            )
            to += unit
    for copy in copies:
        copy.start()
    for copy in copies:
        copy.wait()


def carve(spot, weight, local, cols, parts):
    rows = sum(part[2] for part in parts)
    return pl.pallas_call(
        functools.partial(carve_kernel, local, cols, parts),
        out_shape=jax.ShapeDtypeStruct((rows, cols), weight.dtype),
        in_specs=[SMEM, ANY],
        out_specs=VMEM,
        scratch_shapes=[pltpu.SemaphoreType.DMA((rows // (HD // 2),))],
        compiler_params=limit(4),
        name="carve",
    )(spot, in_hbm(weight))


def absorb_kernel(heads, count, first, last, *refs):
    q_refs, kv_refs, rest = refs[:2], refs[2 : 2 + count], refs[2 + count :]
    state = None if first else rest[0]
    outs = rest if first else rest[1:]
    keys = kv_refs[0].shape[1]
    factor = LOG2E / math.sqrt(HD)
    for place, head in enumerate(heads):
        base = place * 2 * HD
        key = jnp.concatenate(
            [
                kv[base : base + HD, piece * HD : (piece + 1) * HD]
                for kv in kv_refs
                for piece in range(keys // HD)
            ],
            axis=0,
        )
        value = jnp.concatenate([kv[base + HD : base + 2 * HD, :] for kv in kv_refs], axis=1)
        tall = jnp.concatenate([value, jnp.ones((16, value.shape[1]), jnp.bfloat16)], axis=0)
        for side, q_ref in enumerate(q_refs):
            query = q_ref[head * HD : (head + 1) * HD, :]
            scores = jnp.dot(key, query, preferred_element_type=jnp.float32)
            top = jnp.max(scores, axis=0, keepdims=True)
            if not first:
                top_old = state[place, side, HD + 8 : HD + 9, :]
                top = jnp.maximum(top_old, top)
            raised = jnp.exp2((scores - top) * factor).astype(jnp.bfloat16)
            both = jnp.dot(tall, raised, preferred_element_type=jnp.float32)
            mixed, total = both[:HD], both[HD : HD + 8]
            if not first:
                shrink = jnp.exp2((top_old - top) * factor)
                mixed = state[place, side, :HD, :] * shrink + mixed
                total = state[place, side, HD : HD + 8, :] * shrink + total
            if last:
                done = mixed * (1.0 / total[:1])
                outs[side][:, place * HD : (place + 1) * HD] = done.T.astype(jnp.bfloat16)
            else:
                outs[0][place, side, :HD, :] = mixed
                outs[0][place, side, HD : HD + 8, :] = total
                outs[0][place, side, HD + 8 :, :] = jnp.broadcast_to(top, total.shape)


def absorb(asking, blocks, heads, state, last):
    rows = asking[0].shape[1]
    keys = blocks[0].shape[1] * len(blocks)
    count = len(heads)
    first = state is None
    if last:
        shape = jax.ShapeDtypeStruct((rows, count * HD), jnp.bfloat16)
        out_shape, out_specs = (shape, shape), (VMEM, VMEM)
    else:
        out_shape = jax.ShapeDtypeStruct((count, 2, STATE, rows), jnp.float32)
        out_specs = VMEM
    operands = [*asking, *blocks] + ([] if first else [state])
    return pl.pallas_call(
        functools.partial(absorb_kernel, heads, len(blocks), first, last),
        out_shape=out_shape,
        in_specs=[VMEM] * len(operands),
        out_specs=out_specs,
        input_output_aliases={} if first or last else {len(operands) - 1: 0},
        cost_estimate=pl.CostEstimate(
            flops=8 * count * rows * keys * HD,
            bytes_accessed=count * rows * HD * 12,
            transcendentals=2 * count * rows * keys,
        ),
        compiler_params=limit(12),
        name="absorb",
    )(*operands)


def base_kernel(wide, spot_ref, ours, third, back, weight, stream, gate, out, kept):
    left = jnp.concatenate([ours[...], third[...], back[...]], axis=1)
    depth = left.shape[1]
    cols = out.shape[1]
    for at in range(cols // wide):
        lanes = slice(at * wide, (at + 1) * wide)
        scale = gate[:, pl.ds(pl.multiple_of(spot_ref[1] * cols + at * wide, HD), wide)]
        branch = jnp.dot(left, weight[:depth, lanes], preferred_element_type=jnp.float32)
        out[:, lanes] = stream[:, lanes].astype(jnp.float32) + scale * branch
        kept[:, lanes] = scale


def first_base(spot, ours, third, back, weight, stream, gate, wide):
    rows, cols = stream.shape
    return pl.pallas_call(
        functools.partial(base_kernel, wide),
        out_shape=(
            jax.ShapeDtypeStruct((rows, cols), jnp.float32),
            jax.ShapeDtypeStruct((1, cols), gate.dtype),
        ),
        in_specs=[SMEM] + [VMEM] * 6,
        out_specs=(VMEM, VMEM),
        cost_estimate=pl.CostEstimate(
            flops=10 * HD * rows * cols, bytes_accessed=rows * cols * 4, transcendentals=0
        ),
        compiler_params=limit(12),
        name="first_base",
    )(spot, ours, third, back, weight, stream, gate)


def middle_kernel(wide, over, cross, passed, relayed, others, base, gate, out):
    left = jnp.concatenate([over[...], cross[...]], axis=1)
    half = others.shape[0] // 2
    for at in range(base.shape[1] // wide):
        lanes = slice(at * wide, (at + 1) * wide)
        right = jnp.concatenate(
            [
                passed[HD:, lanes],
                others[:half, lanes],
                relayed[HD:, lanes],
                others[half:, lanes],
            ],
            axis=0,
        )
        branch = jnp.dot(left, right, preferred_element_type=jnp.float32)
        out[:, lanes] = base[:, lanes] + gate[:, lanes] * branch


def middle(over, cross, passed, relayed, others, base, gate, wide):
    return pl.pallas_call(
        functools.partial(middle_kernel, wide),
        out_shape=jax.ShapeDtypeStruct(base.shape, jnp.float32),
        in_specs=[VMEM] * 7,
        out_specs=VMEM,
        input_output_aliases={5: 0},
        cost_estimate=pl.CostEstimate(
            flops=8 * HD * base.size, bytes_accessed=base.size, transcendentals=0
        ),
        compiler_params=limit(12),
        name="middle",
    )(over, cross, passed, relayed, others, base, gate)


def finish_kernel(pieces, wide, *refs):
    lefts, rights = refs[:pieces], refs[pieces : 2 * pieces]
    base, gate, out, held, sems = refs[2 * pieces :]
    left = jnp.concatenate([ref[...] for ref in lefts], axis=1)
    copies = []
    for at in range(base.shape[1] // wide):
        lanes = slice(at * wide, (at + 1) * wide)
        right = jnp.concatenate(
            [rights[0][-HD:, lanes]] + [ref[:HD, lanes] for ref in rights[1:]], axis=0
        )
        branch = jnp.dot(left, right, preferred_element_type=jnp.float32)
        held[:, lanes] = (base[:, lanes] + gate[:, lanes] * branch).astype(held.dtype)
        copies.append(pltpu.make_async_copy(held.at[:, lanes], out.at[:, lanes], sems.at[at]))
        copies[-1].start()
    for copy in copies:
        copy.wait()


def finish(pieces, weights, base, gate, wide):
    operands = [*pieces, *weights, base, gate]
    return pl.pallas_call(
        functools.partial(finish_kernel, len(pieces), wide),
        out_shape=jax.ShapeDtypeStruct(base.shape, jnp.bfloat16),
        in_specs=[VMEM] * len(operands),
        out_specs=ANY,
        scratch_shapes=[
            pltpu.VMEM(base.shape, jnp.bfloat16),
            pltpu.SemaphoreType.DMA((base.shape[1] // wide,)),
        ],
        cost_estimate=pl.CostEstimate(
            flops=2 * len(pieces) * HD * base.size, bytes_accessed=base.size * 2, transcendentals=0
        ),
        compiler_params=limit(12),
        name="finish",
    )(*operands)


def role_of(member):
    return member // 2 % 2


def per_device(stream_in, queries, keys, values, out_weight, gate_scale):
    sections = lax.axis_size("segment")
    seq_count = lax.axis_size("seq")
    shares = lax.axis_size("head")
    local = queries.shape[2] // HD // 2
    cycle_len = min(32, seq_count)
    stride = seq_count // cycle_len
    planes = cycle_len // 2
    rounds = planes // 2

    partner = {m: m ^ 2 for m in range(cycle_len)}
    beside = {m: m ^ 1 for m in range(cycle_len)}
    beyond = {}
    for role in range(2):
        for column in range(2):
            line = [p * 2 + column for p in range(planes) if role_of(p * 2) == role]
            for at, m in enumerate(line):
                beyond[m] = line[(at + 1) % len(line)]

    def hop(block, towards, shift=0, by=0):
        pairs = []
        for section in range(sections):
            for member in range(cycle_len):
                for video in range(stride):
                    for share in range(shares):
                        origin = section * seq_count + member * stride + video
                        target = (
                            (section + shift) % sections * seq_count
                            + towards[member] * stride
                            + video
                        )
                        pairs.append(
                            (origin * shares + share, target * shares + (share + by) % shares)
                        )
        return lax.ppermute(block, ("segment", "seq", "head"), pairs)

    still = {m: m for m in range(cycle_len)}
    share = lax.axis_index("head").astype(jnp.int32)
    role = role_of(lax.axis_index("seq").astype(jnp.int32) // stride)
    groups = [(0, 1), (2,)]

    col_count = out_weight.shape[2] // shares
    spots = {by: jnp.stack([role, lax.rem(share + by, shares)]) for by in range(1, shares)}
    packed = pack(
        spots[1], keys[0], values[0], queries[0], out_weight[0], groups, col_count
    )
    mine, give = packed[: len(groups)], packed[len(groups) : 2 * len(groups)]
    my_query, give_query, own_thirds = packed[-3:]
    got = [None] * len(groups)
    far = [[None] * 2 for _ in groups]
    near = [[None] * 2 for _ in groups]
    own = [None] * len(groups)
    everyone = range(len(groups))
    for g in everyone:
        got[g] = hop(give[g], partner, 1)
        far[g][0] = hop(mine[g], beyond, 1)
        near[g][0] = hop(mine[g], beside, 1)
        own[g] = hop(mine[g], still, 1)
    asking = [hop(my_query, still, 1), hop(give_query, partner, 1)]

    lent = {}
    rest = 2 * HD - SHARED
    for by in range(1, shares):
        part = own_thirds
        if by > 1:
            wanted = ((True, 2 * HD, HD), (True, 0, SHARED))
            part = carve(spots[by], out_weight[0], local, col_count, wanted)
        passed = hop(part, still, 1, by)
        wanted = ((True, SHARED, rest), (False, SHARED, rest))
        part = carve(spots[by], out_weight[0], local, col_count, wanted)
        lent[by] = (passed, hop(passed, partner), hop(part, still, 1, by))
    here = jnp.stack([role, share])
    kept = carve(
        here, out_weight[0], local, col_count, ((True, 0, local * HD), (False, 0, local * HD))
    )
    lines = carve(
        here * jnp.array([0, 1], jnp.int32),
        stream_in[0],
        local,
        col_count,
        ((True, 0, stream_in.shape[1]),),
    )
    weight = hop(kept, still, 1)
    stream = hop(lines, still, 1)
    gate = hop(gate_scale, still, 1)

    def fold(g, blocks, held, last=False):
        return absorb(asking, blocks, groups[g], held, last)

    attended = []
    for g in everyone:
        far[g][1] = hop(got[g], beyond)
        near[g][1] = hop(got[g], beside)
        state = fold(g, [own[g], got[g], *near[g]], None)
        arrived = far[g]
        for turn in range(1, rounds):
            onward = [hop(arrived[i], beside) for i in range(2)]
            state = fold(g, [arrived[0], onward[0]], state)
            state = fold(g, arrived[1:], state)
            if turn < rounds - 1:
                state = fold(g, onward[1:], state)
                arrived = [hop(arrived[i], beyond) for i in range(2)]
            else:
                attended.append(fold(g, onward[1:], state, True))

    home = []
    for g in everyone:
        ours, theirs = attended[g]
        back = hop(theirs, partner)
        over = {by: hop(ours, still, 0, by) for by in range(1, shares)}
        cross = {by: hop(theirs, partner, 0, by) for by in range(1, shares)}
        home.append((ours, back, over, cross))

    first, second = home
    base, own_gate = first_base(
        here, first[0], second[0], first[1], weight, stream, gate, 512
    )
    last_pieces, last_weights = [second[1]], [weight]
    for by in range(1, shares):
        passed, relayed, others = lent[by]
        base = middle(
            first[2][by], first[3][by], passed, relayed, others, base, own_gate, 512
        )
        last_pieces += [second[2][by], second[3][by]]
        last_weights += [passed, relayed]
    return finish(last_pieces, last_weights, base, own_gate, 384)[None]


def solution(mesh):
    return jax.shard_map(
        per_device,
        mesh=mesh,
        in_specs=(
            P("segment", "seq", None),
            P("segment", "seq", "head"),
            P("segment", "seq", "head"),
            P("segment", "seq", "head"),
            P("segment", "head", None),
            P("segment", None),
        ),
        out_specs=P("segment", "seq", "head"),
        check_vma=False,
    )
```

```python
import functools
import math

import jax
import jax.numpy as jnp
from jax import lax
from jax.experimental import pallas as pl
from jax.experimental.pallas import tpu as pltpu
from jax.sharding import PartitionSpec as P


HD = 128
STATE = HD + 16
SHARED = 32
LOG2E = 1.4426950408889634
VMEM = pl.BlockSpec(memory_space=pltpu.VMEM)


def limit(mib):
    return pltpu.CompilerParams(vmem_limit_bytes=mib << 20)


def pack_kernel(groups, local, cols, spot_ref, k_any, v_any, q_any, w_any, *rest):
    outs, (k_ref, v_ref, q_ref, sems) = rest[:-4], rest[-4:]
    mine_role = spot_ref[0]
    lanes = pl.ds(pl.multiple_of(spot_ref[1] * cols, HD), cols)
    third = w_any.at[pl.ds(pl.multiple_of((mine_role * local + 2) * HD, HD), HD), lanes]
    start = w_any.at[pl.ds(pl.multiple_of(mine_role * local * HD, HD), SHARED), lanes]
    loads = [
        pltpu.make_async_copy(source, target, sems.at[at])
        for at, (source, target) in enumerate(
            (
                (k_any, k_ref),
                (v_any, v_ref),
                (q_any, q_ref),
                (third, outs[-1].at[:HD, :]),
                (start, outs[-1].at[HD:, :]),
            )
        )
    ]
    for load in loads:
        load.start()
    rows, width = k_ref.shape
    half = width // 2
    loads[0].wait()
    loads[1].wait()
    for side in range(2):
        role = mine_role if side == 0 else 1 - mine_role
        for heads, out in zip(groups, outs[side * len(groups) :]):
            for place, head in enumerate(heads):
                lanes = pl.ds(pl.multiple_of(role * half + head * HD, HD), HD)
                base = place * 2 * HD
                for piece in range(rows // HD):
                    out[base : base + HD, piece * HD : (piece + 1) * HD] = k_ref[
                        piece * HD : (piece + 1) * HD, lanes
                    ]
                out[base + HD : base + 2 * HD, :] = v_ref[:, lanes].T
    loads[2].wait()
    for side in range(2):
        role = mine_role if side == 0 else 1 - mine_role
        for head in range(half // HD):
            lanes = pl.ds(pl.multiple_of(role * half + head * HD, HD), HD)
            outs[side - 3][head * HD : (head + 1) * HD, :] = q_ref[:, lanes].T
    loads[3].wait()
    loads[4].wait()


SMEM = pl.BlockSpec(memory_space=pltpu.SMEM)
ANY = pl.BlockSpec(memory_space=pl.ANY)


def in_hbm(x):
    return pltpu.with_memory_space_constraint(x, pltpu.HBM)


def pack(spot, keys, values, queries, weight, groups, cols):
    rows, width = keys.shape
    shapes = [
        jax.ShapeDtypeStruct((len(heads) * 2 * HD, rows), jnp.bfloat16) for heads in groups
    ]
    asked = jax.ShapeDtypeStruct((width // 2, rows), jnp.bfloat16)
    third = jax.ShapeDtypeStruct((HD + SHARED, cols), jnp.bfloat16)
    return pl.pallas_call(
        functools.partial(pack_kernel, groups, width // 2 // HD, cols),
        out_shape=tuple(shapes + shapes + [asked, asked, third]),
        in_specs=[SMEM, ANY, ANY, ANY, ANY],
        out_specs=(VMEM,) * (2 * len(groups) + 3),
        scratch_shapes=[pltpu.VMEM((rows, width), jnp.bfloat16)] * 3
        + [pltpu.SemaphoreType.DMA((5,))],
        compiler_params=limit(8),
        name="pack",
    )(spot, in_hbm(keys), in_hbm(values), in_hbm(queries), in_hbm(weight))


def carve_kernel(local, cols, parts, spot_ref, w_any, *rest):
    out, sems = rest
    lanes = pl.ds(pl.multiple_of(spot_ref[1] * cols, HD), cols)
    unit = HD // 4
    copies, to = [], 0
    for ours, first, count in parts:
        role = spot_ref[0] if ours else 1 - spot_ref[0]
        for at in range(first, first + count, unit):
            row = pl.multiple_of(role * local * HD + at, unit)
            copies.append(
                pltpu.make_async_copy(
                    w_any.at[pl.ds(row, unit), lanes],
                    out.at[to : to + unit, :],
                    sems.at[len(copies)],
                )
            )
            to += unit
    for copy in copies:
        copy.start()
    for copy in copies:
        copy.wait()


def carve(spot, weight, local, cols, parts):
    rows = sum(part[2] for part in parts)
    return pl.pallas_call(
        functools.partial(carve_kernel, local, cols, parts),
        out_shape=jax.ShapeDtypeStruct((rows, cols), weight.dtype),
        in_specs=[SMEM, ANY],
        out_specs=VMEM,
        scratch_shapes=[pltpu.SemaphoreType.DMA((rows // (HD // 4),))],
        compiler_params=limit(4),
        name="carve",
    )(spot, in_hbm(weight))


def absorb_kernel(heads, count, first, last, *refs):
    q_refs, kv_refs, rest = refs[:2], refs[2 : 2 + count], refs[2 + count :]
    state = None if first else rest[0]
    outs = rest if first else rest[1:]
    keys = kv_refs[0].shape[1]
    factor = LOG2E / math.sqrt(HD)
    for place, head in enumerate(heads):
        base = place * 2 * HD
        key = jnp.concatenate(
            [
                kv[base : base + HD, piece * HD : (piece + 1) * HD]
                for kv in kv_refs
                for piece in range(keys // HD)
            ],
            axis=0,
        )
        value = jnp.concatenate([kv[base + HD : base + 2 * HD, :] for kv in kv_refs], axis=1)
        tall = jnp.concatenate([value, jnp.ones((16, value.shape[1]), jnp.bfloat16)], axis=0)
        for side, q_ref in enumerate(q_refs):
            query = q_ref[head * HD : (head + 1) * HD, :]
            scores = jnp.dot(key, query, preferred_element_type=jnp.float32)
            top = jnp.max(scores, axis=0, keepdims=True)
            if not first:
                top_old = state[place, side, HD + 8 : HD + 9, :]
                top = jnp.maximum(top_old, top)
            raised = jnp.exp2((scores - top) * factor).astype(jnp.bfloat16)
            both = jnp.dot(tall, raised, preferred_element_type=jnp.float32)
            mixed, total = both[:HD], both[HD : HD + 8]
            if not first:
                shrink = jnp.exp2((top_old - top) * factor)
                mixed = state[place, side, :HD, :] * shrink + mixed
                total = state[place, side, HD : HD + 8, :] * shrink + total
            if last:
                done = mixed / total[:1]
                outs[side][:, place * HD : (place + 1) * HD] = done.T.astype(jnp.bfloat16)
            else:
                outs[0][place, side, :HD, :] = mixed
                outs[0][place, side, HD : HD + 8, :] = total
                outs[0][place, side, HD + 8 :, :] = jnp.broadcast_to(top, total.shape)


def absorb(asking, blocks, heads, state, last):
    rows = asking[0].shape[1]
    keys = blocks[0].shape[1] * len(blocks)
    count = len(heads)
    first = state is None
    if last:
        shape = jax.ShapeDtypeStruct((rows, count * HD), jnp.bfloat16)
        out_shape, out_specs = (shape, shape), (VMEM, VMEM)
    else:
        out_shape = jax.ShapeDtypeStruct((count, 2, STATE, rows), jnp.float32)
        out_specs = VMEM
    operands = [*asking, *blocks] + ([] if first else [state])
    return pl.pallas_call(
        functools.partial(absorb_kernel, heads, len(blocks), first, last),
        out_shape=out_shape,
        in_specs=[VMEM] * len(operands),
        out_specs=out_specs,
        input_output_aliases={} if first or last else {len(operands) - 1: 0},
        cost_estimate=pl.CostEstimate(
            flops=8 * count * rows * keys * HD,
            bytes_accessed=count * rows * HD * 12,
            transcendentals=2 * count * rows * keys,
        ),
        compiler_params=limit(12),
        name="absorb",
    )(*operands)


def base_kernel(wide, spot_ref, ours, third, back, weight, stream, gate, out, kept):
    left = jnp.concatenate([ours[...], third[...], back[...]], axis=1)
    depth = left.shape[1]
    cols = out.shape[1]
    for at in range(cols // wide):
        lanes = slice(at * wide, (at + 1) * wide)
        scale = gate[:, pl.ds(pl.multiple_of(spot_ref[1] * cols + at * wide, HD), wide)]
        branch = jnp.dot(left, weight[:depth, lanes], preferred_element_type=jnp.float32)
        out[:, lanes] = stream[:, lanes].astype(jnp.float32) + scale * branch
        kept[:, lanes] = scale


def first_base(spot, ours, third, back, weight, stream, gate, wide):
    rows, cols = stream.shape
    return pl.pallas_call(
        functools.partial(base_kernel, wide),
        out_shape=(
            jax.ShapeDtypeStruct((rows, cols), jnp.float32),
            jax.ShapeDtypeStruct((1, cols), gate.dtype),
        ),
        in_specs=[SMEM] + [VMEM] * 6,
        out_specs=(VMEM, VMEM),
        cost_estimate=pl.CostEstimate(
            flops=10 * HD * rows * cols, bytes_accessed=rows * cols * 4, transcendentals=0
        ),
        compiler_params=limit(12),
        name="first_base",
    )(spot, ours, third, back, weight, stream, gate)


def middle_kernel(wide, over, cross, passed, relayed, others, base, gate, out):
    left = jnp.concatenate([over[...], cross[...]], axis=1)
    half = others.shape[0] // 2
    for at in range(base.shape[1] // wide):
        lanes = slice(at * wide, (at + 1) * wide)
        right = jnp.concatenate(
            [
                passed[HD:, lanes],
                others[:half, lanes],
                relayed[HD:, lanes],
                others[half:, lanes],
            ],
            axis=0,
        )
        branch = jnp.dot(left, right, preferred_element_type=jnp.float32)
        out[:, lanes] = base[:, lanes] + gate[:, lanes] * branch


def middle(over, cross, passed, relayed, others, base, gate, wide):
    return pl.pallas_call(
        functools.partial(middle_kernel, wide),
        out_shape=jax.ShapeDtypeStruct(base.shape, jnp.float32),
        in_specs=[VMEM] * 7,
        out_specs=VMEM,
        input_output_aliases={5: 0},
        cost_estimate=pl.CostEstimate(
            flops=8 * HD * base.size, bytes_accessed=base.size, transcendentals=0
        ),
        compiler_params=limit(12),
        name="middle",
    )(over, cross, passed, relayed, others, base, gate)


def finish_kernel(pieces, wide, *refs):
    lefts, rights = refs[:pieces], refs[pieces : 2 * pieces]
    base, gate, out, held, sems = refs[2 * pieces :]
    left = jnp.concatenate([ref[...] for ref in lefts], axis=1)
    copies = []
    for at in range(base.shape[1] // wide):
        lanes = slice(at * wide, (at + 1) * wide)
        right = jnp.concatenate(
            [rights[0][-HD:, lanes]] + [ref[:HD, lanes] for ref in rights[1:]], axis=0
        )
        branch = jnp.dot(left, right, preferred_element_type=jnp.float32)
        held[:, lanes] = (base[:, lanes] + gate[:, lanes] * branch).astype(held.dtype)
        copies.append(pltpu.make_async_copy(held.at[:, lanes], out.at[:, lanes], sems.at[at]))
        copies[-1].start()
    for copy in copies:
        copy.wait()


def finish(pieces, weights, base, gate, wide):
    operands = [*pieces, *weights, base, gate]
    return pl.pallas_call(
        functools.partial(finish_kernel, len(pieces), wide),
        out_shape=jax.ShapeDtypeStruct(base.shape, jnp.bfloat16),
        in_specs=[VMEM] * len(operands),
        out_specs=ANY,
        scratch_shapes=[
            pltpu.VMEM(base.shape, jnp.bfloat16),
            pltpu.SemaphoreType.DMA((base.shape[1] // wide,)),
        ],
        cost_estimate=pl.CostEstimate(
            flops=2 * len(pieces) * HD * base.size, bytes_accessed=base.size * 2, transcendentals=0
        ),
        compiler_params=limit(12),
        name="finish",
    )(*operands)


def role_of(member):
    return member // 2 % 2


def per_device(stream_in, queries, keys, values, out_weight, gate_scale):
    sections = lax.axis_size("segment")
    seq_count = lax.axis_size("seq")
    shares = lax.axis_size("head")
    local = queries.shape[2] // HD // 2
    cycle_len = min(32, seq_count)
    stride = seq_count // cycle_len
    planes = cycle_len // 2
    rounds = planes // 2

    partner = {m: m ^ 2 for m in range(cycle_len)}
    beside = {m: m ^ 1 for m in range(cycle_len)}
    beyond = {}
    for role in range(2):
        for column in range(2):
            line = [p * 2 + column for p in range(planes) if role_of(p * 2) == role]
            for at, m in enumerate(line):
                beyond[m] = line[(at + 1) % len(line)]

    def hop(block, towards, shift=0, by=0):
        pairs = []
        for section in range(sections):
            for member in range(cycle_len):
                for video in range(stride):
                    for share in range(shares):
                        origin = section * seq_count + member * stride + video
                        target = (
                            (section + shift) % sections * seq_count
                            + towards[member] * stride
                            + video
                        )
                        pairs.append(
                            (origin * shares + share, target * shares + (share + by) % shares)
                        )
        return lax.ppermute(block, ("segment", "seq", "head"), pairs)

    still = {m: m for m in range(cycle_len)}
    share = lax.axis_index("head").astype(jnp.int32)
    role = role_of(lax.axis_index("seq").astype(jnp.int32) // stride)
    groups = [(0, 1), (2,)]

    col_count = out_weight.shape[2] // shares
    spots = {by: jnp.stack([role, lax.rem(share + by, shares)]) for by in range(1, shares)}
    packed = pack(
        spots[1], keys[0], values[0], queries[0], out_weight[0], groups, col_count
    )
    mine, give = packed[: len(groups)], packed[len(groups) : 2 * len(groups)]
    my_query, give_query, own_thirds = packed[-3:]
    got = [None] * len(groups)
    far = [[None] * 2 for _ in groups]
    near = [[None] * 2 for _ in groups]
    own = [None] * len(groups)
    everyone = range(len(groups))
    for g in everyone:
        got[g] = hop(give[g], partner, 1)
        far[g][0] = hop(mine[g], beyond, 1)
        near[g][0] = hop(mine[g], beside, 1)
        own[g] = hop(mine[g], still, 1)
    asking = [hop(my_query, still, 1), hop(give_query, partner, 1)]

    lent = {}
    rest = 2 * HD - SHARED
    for by in range(1, shares):
        part = own_thirds
        if by > 1:
            wanted = ((True, 2 * HD, HD), (True, 0, SHARED))
            part = carve(spots[by], out_weight[0], local, col_count, wanted)
        passed = hop(part, still, 1, by)
        wanted = ((True, SHARED, rest), (False, SHARED, rest))
        part = carve(spots[by], out_weight[0], local, col_count, wanted)
        lent[by] = (passed, hop(passed, partner), hop(part, still, 1, by))
    here = jnp.stack([role, share])
    kept = carve(
        here, out_weight[0], local, col_count, ((True, 0, local * HD), (False, 0, local * HD))
    )
    lines = carve(
        here * jnp.array([0, 1], jnp.int32),
        stream_in[0],
        local,
        col_count,
        ((True, 0, stream_in.shape[1]),),
    )
    weight = hop(kept, still, 1)
    stream = hop(lines, still, 1)
    gate = hop(gate_scale, still, 1)

    def fold(g, blocks, held, last=False):
        return absorb(asking, blocks, groups[g], held, last)

    attended = []
    for g in everyone:
        far[g][1] = hop(got[g], beyond)
        near[g][1] = hop(got[g], beside)
        state = fold(g, [own[g], got[g], *near[g]], None)
        arrived = far[g]
        for turn in range(1, rounds):
            onward = [hop(arrived[i], beside) for i in range(2)]
            state = fold(g, [arrived[0], onward[0]], state)
            state = fold(g, arrived[1:], state)
            if turn < rounds - 1:
                state = fold(g, onward[1:], state)
                arrived = [hop(arrived[i], beyond) for i in range(2)]
            else:
                attended.append(fold(g, onward[1:], state, True))

    home = []
    for g in everyone:
        ours, theirs = attended[g]
        back = hop(theirs, partner)
        over = {by: hop(ours, still, 0, by) for by in range(1, shares)}
        cross = {by: hop(theirs, partner, 0, by) for by in range(1, shares)}
        home.append((ours, back, over, cross))

    first, second = home
    base, own_gate = first_base(
        here, first[0], second[0], first[1], weight, stream, gate, 512
    )
    last_pieces, last_weights = [second[1]], [weight]
    for by in range(1, shares):
        passed, relayed, others = lent[by]
        base = middle(
            first[2][by], first[3][by], passed, relayed, others, base, own_gate, 512
        )
        last_pieces += [second[2][by], second[3][by]]
        last_weights += [passed, relayed]
    return finish(last_pieces, last_weights, base, own_gate, 384)[None]


def solution(mesh):
    return jax.shard_map(
        per_device,
        mesh=mesh,
        in_specs=(
            P("segment", "seq", None),
            P("segment", "seq", "head"),
            P("segment", "seq", "head"),
            P("segment", "seq", "head"),
            P("segment", "head", None),
            P("segment", None),
        ),
        out_specs=P("segment", "seq", "head"),
        check_vma=False,
    )
```
